32 devices in a mesh: bag: 4 (over x, core), sp: 8 (over z, y).
Axes of the slice: x: 2, y: 2, z: 4, core: 2. Of those that a mesh axis runs over, the one named last changes fastest.
Arguments:
- tokens: bfloat16 [8192, 1152], P(('bag', 'sp')), may hold values from -8 to 8
- row_seq: int32 [8192], P(('bag', 'sp')), may hold values from 0 to 3, as said below
- modulation: float32 [4, 6, 1152], replicated, may hold values from -4 to 4
- w_qkv: bfloat16 [1152, 3456], replicated, may hold values from -1 to 1
- w_out: bfloat16 [1152, 1152], replicated, may hold values from -0.1875 to 0.1875
- w_fc1: bfloat16 [1152, 2304], replicated, may hold values from -0.1875 to 0.1875
- w_fc2: bfloat16 [2304, 1152], replicated, may hold values from -0.125 to 0.125
Outputs:
- output: bfloat16 [8192, 1152], P(('bag', 'sp'))
The draws below stay inside these ranges and needn't reach their ends.
Inputs may be any that keep to these rules, and one draw needn't show every extreme that they name: `row_seq`: rows 2m and 2m + 1 belong to the same sequence. Sequence s lies in bag s. Of one device's 256 rows at most 80 lie in any one bag, and on every device exactly 80 lie in one bag. Every sequence has rows.
All inputs are finite; a program needn't handle non-finite values.
Results may differ from the reference program's by a relative error of at most 0.0095.
Values may be sent and summed in bfloat16 or wider, within the bound.
No kernel may reach another device: no remote copies, remote signals or barrier semaphores. Data moves between devices by JAX's collectives and lax.ppermute only.
A program may use at most 128 MiB of HBM per device.

```python
import math
import jax
import jax.numpy as jnp
from jax import lax

D = 1152
H = 16
HD = 72
FF = 2304
SEQ_BAG = 1
ROWS_DEV = 256
BAG_SLOTS = 2560
SEQS = 4
TOKENS = 8192
N_BAG = 4
N_SP = 8


def draw_row_seq(key, part):
    base_key = jax.random.fold_in(key, 5)
    key_list = jax.random.split(base_key, 6)
    device_total = N_BAG * N_SP
    pair_count = ROWS_DEV // 2
    mean_pairs = pair_count // N_BAG
    extra = mean_pairs // 4
    bag_perms = jax.vmap(lambda one_key: jax.random.permutation(one_key, N_BAG))(jax.random.split(key_list[0], device_total))
    shifted = jax.random.randint(key_list[1], (device_total,), 0, max(extra, 1))
    bag_ids = jnp.arange(N_BAG, dtype=jnp.int32)

    def one_hot(column):
        return (bag_perms[:, column][:, None] == bag_ids[None, :]).astype(jnp.int32)
    counts = mean_pairs + extra * (one_hot(0) - one_hot(1)) + shifted[:, None] * (one_hot(2) - one_hot(3))
    ends = jnp.cumsum(counts, axis=1)
    pair_ids = jnp.arange(pair_count, dtype=jnp.int32)
    bag_of_pair = jnp.sum((pair_ids[None, :, None] >= ends[:, None, :]).astype(jnp.int32), axis=-1)
    pair_perms = jax.vmap(lambda one_key: jax.random.permutation(one_key, pair_count))(jax.random.split(key_list[2], device_total))
    bag_of_pair = jnp.take_along_axis(bag_of_pair, pair_perms, axis=1)
    first_pick = jax.random.randint(key_list[3], (device_total, pair_count), 0, SEQ_BAG)
    second_pick = jax.random.randint(key_list[4], (device_total, pair_count), 0, SEQ_BAG)
    within = jnp.minimum(first_pick, second_pick)
    seq_perms = jax.vmap(lambda one_key: jax.random.permutation(one_key, SEQ_BAG))(jax.random.split(key_list[5], N_BAG))
    local_seq = seq_perms[bag_of_pair, within]
    seq_ids = (bag_of_pair * SEQ_BAG + local_seq).astype(jnp.int32)
    return jnp.repeat(seq_ids, 2, axis=1).reshape(TOKENS).astype(jnp.int32)


def draw_tokens(key, part):
    base = jnp.clip(jax.random.normal(jax.random.fold_in(key, 11), (TOKENS, D), jnp.float32), -6.0, 6.0)
    return base.astype(jnp.bfloat16)


def draw_modulation(key, part):
    table = 0.5 * jnp.clip(jax.random.normal(jax.random.fold_in(key, 21), (SEQS, 6, D), jnp.float32), -6.0, 6.0)
    return table


def draw_w_qkv(key, part):
    matrix = jnp.clip(jax.random.normal(jax.random.fold_in(key, 31), (D, 3, D), jnp.float32), -6.0, 6.0) / jnp.sqrt(jnp.float32(D))
    return matrix.reshape(D, 3 * D).astype(jnp.bfloat16)


def scatter_about(key, dims, scale, limit, kind=jnp.bfloat16):
    result = scale * jax.random.normal(key, dims, jnp.float32)
    return jnp.clip(result, min=-limit, max=limit).astype(kind)


def setup_inputs(seed: int = 0) -> dict:
    seeds = jax.random.split(jax.random.key(seed), 8)
    return {
        "tokens": draw_tokens(jax.random.fold_in(seeds[7], 71), 0),
        "row_seq": draw_row_seq(jax.random.fold_in(seeds[7], 71), 0),
        "modulation": draw_modulation(jax.random.fold_in(seeds[7], 71), 0),
        "w_qkv": draw_w_qkv(jax.random.fold_in(seeds[7], 71), 0),
        "w_out": scatter_about(seeds[4], (D, D), D ** -0.5, 0.1875),
        "w_fc1": scatter_about(seeds[5], (D, FF), D ** -0.5, 0.1875),
        "w_fc2": scatter_about(seeds[6], (FF, D), FF ** -0.5, 0.125),
    }


EPS = 1e-06

def layer_norm(values):
    center = values - lax.optimization_barrier(jnp.mean(values, axis=-1, keepdims=True))
    spread = lax.optimization_barrier(jnp.mean(center * center, axis=-1, keepdims=True))
    return center * lax.rsqrt(spread + EPS)

def reference(tokens, row_seq, modulation, w_qkv, w_out, w_fc1, w_fc2):
    total_rows = tokens.shape[0]

    def per_row(column):
        return jnp.take(modulation[:, column, :], row_seq, axis=0)
    normed1 = (layer_norm(tokens.astype(jnp.float32)) * (1.0 + per_row(1)) + per_row(0)).astype(jnp.bfloat16)
    qkv = jnp.dot(normed1, w_qkv, preferred_element_type=jnp.float32).astype(jnp.bfloat16)
    order = jnp.argsort(row_seq, stable=True).astype(jnp.int32)
    seq_sorted = jnp.take(row_seq, order)
    qkv_sorted = jnp.take(qkv, order, axis=0).reshape(total_rows, 3, H, HD)
    member = (row_seq[:, None] == jnp.arange(SEQS, dtype=jnp.int32)[None, :]).astype(jnp.int32)
    counts = lax.optimization_barrier(jnp.sum(member, axis=0))
    starts = (jnp.cumsum(counts) - counts).astype(jnp.int32)
    block_size = math.gcd(total_rows, 512)
    window = min(total_rows, 2 * BAG_SLOTS + block_size)
    score_scale = 1.0 / math.sqrt(HD)

    def one_block(block_index):
        first_row = (block_index * block_size).astype(jnp.int32)
        query_part = lax.dynamic_slice_in_dim(qkv_sorted, first_row, block_size, 0)
        query_seq = lax.dynamic_slice_in_dim(seq_sorted, first_row, block_size, 0)
        key_start = jnp.minimum(starts[query_seq[0]], total_rows - window).astype(jnp.int32)
        key_part = lax.dynamic_slice_in_dim(qkv_sorted, key_start, window, 0)
        key_seq = lax.dynamic_slice_in_dim(seq_sorted, key_start, window, 0)
        queries = query_part[:, 0].astype(jnp.float32)
        key_rows = key_part[:, 1].astype(jnp.float32)
        values = key_part[:, 2].astype(jnp.float32)
        scores = jnp.einsum('qhd,khd->hqk', queries, key_rows) * score_scale
        allowed = query_seq[:, None] == key_seq[None, :]
        scores = jnp.where(allowed[None], scores, -jnp.inf)
        row_max = lax.optimization_barrier(jnp.max(scores, axis=-1, keepdims=True))
        raised = jnp.exp(scores - row_max)
        denominator = lax.optimization_barrier(jnp.sum(raised, axis=-1))
        probs = raised.astype(jnp.bfloat16).astype(jnp.float32)
        mixed_rows = jnp.einsum('hqk,khd->qhd', probs, values)
        mixed_rows = mixed_rows / jnp.transpose(denominator)[:, :, None]
        return mixed_rows.astype(jnp.bfloat16).reshape(block_size, D)
    attended_sorted = lax.map(one_block, jnp.arange(total_rows // block_size, dtype=jnp.int32)).reshape(total_rows, D)
    attended = jnp.zeros((total_rows, D), jnp.bfloat16).at[order].set(attended_sorted)
    branch = jnp.dot(attended, w_out, preferred_element_type=jnp.float32)
    hidden = (tokens.astype(jnp.float32) + per_row(2) * branch).astype(jnp.bfloat16)
    normed2 = (layer_norm(hidden.astype(jnp.float32)) * (1.0 + per_row(4)) + per_row(3)).astype(jnp.bfloat16)
    active = jax.nn.gelu(jnp.dot(normed2, w_fc1, preferred_element_type=jnp.float32), approximate=True).astype(jnp.bfloat16)
    return (hidden.astype(jnp.float32) + per_row(5) * jnp.dot(active, w_fc2, preferred_element_type=jnp.float32)).astype(jnp.bfloat16)
```

```python
import functools
import math

import jax
import jax.numpy as jnp
from jax import lax
from jax.experimental import pallas as pl
from jax.experimental.pallas import tpu as pltpu
from jax.sharding import PartitionSpec as P

HD = 72
SEQ_BAG = 1
LANE = 128
EPS = 1e-06
HUGE = 1e30
AXES = ("bag", "sp")
BF16, F32 = jnp.bfloat16, jnp.float32


def vmem():
    return pl.BlockSpec(memory_space=pltpu.VMEM)


def smem():
    return pl.BlockSpec(memory_space=pltpu.SMEM)


def hbm():
    return pl.BlockSpec(memory_space=pl.ANY)


def layer_norm(values):
    center = values - jnp.mean(values, axis=-1, keepdims=True)
    spread = jnp.mean(center * center, axis=-1, keepdims=True)
    return center * lax.rsqrt(spread + EPS)


def to_column(row):
    n = row.shape[1]
    diagonal = lax.broadcasted_iota(jnp.int32, (n, n), 0) == lax.broadcasted_iota(jnp.int32, (n, n), 1)
    return jnp.sum(jnp.where(diagonal, jnp.broadcast_to(row, (n, n)), 0.0), axis=1, keepdims=True)


def slot_of_row(bag_row, capacity):
    n = bag_row.shape[1]
    earlier = lax.broadcasted_iota(jnp.int32, (n, n), 0) < lax.broadcasted_iota(jnp.int32, (n, n), 1)
    same = jnp.broadcast_to(to_column(bag_row), (n, n)) == jnp.broadcast_to(bag_row, (n, n))
    rank = jnp.sum(jnp.where(same & earlier, 1.0, 0.0), axis=0, keepdims=True)
    return (bag_row * capacity + rank).astype(jnp.int32)


def slot_kernel(capacity, place_ref, tokens_ref, seq_ref, mod_ref, *out_refs):
    me = place_ref[0]
    row_count, width = tokens_ref.shape
    block_count = len(out_refs)
    bag_row = ((seq_ref[...] // SEQ_BAG) ^ me).astype(F32)
    position = slot_of_row(bag_row, capacity)
    slot_ids = lax.broadcasted_iota(jnp.int32, (block_count * capacity, row_count), 0)
    pick = jnp.where(slot_ids == position, 1.0, 0.0)
    filled = jnp.sum(pick, axis=1, keepdims=True)
    rows = jnp.dot(pick.astype(BF16), tokens_ref[...], preferred_element_type=F32)
    first = lax.broadcasted_iota(jnp.int32, (capacity, width), 1) == 0
    for block, out_ref in enumerate(out_refs):
        part = slice(block * capacity, (block + 1) * capacity)
        mods = mod_ref[block ^ me]
        normed = layer_norm(rows[part]) * (1.0 + mods[1:2]) + mods[0:1]
        normed = jnp.where(first & (filled[part] < 0.5), HUGE, normed)
        out_ref[...] = normed.astype(BF16)


def slot_rows(place, tokens, seq_row, modulation, bag_count, capacity):
    width = tokens.shape[1]
    return pl.pallas_call(
        functools.partial(slot_kernel, capacity),
        in_specs=[smem(), vmem(), vmem(), vmem()],
        out_specs=[vmem()] * bag_count,
        out_shape=[jax.ShapeDtypeStruct((capacity, width), BF16)] * bag_count,
        name="slot_rows",
    )(place, tokens, seq_row, modulation)


def weight_kernel(head_count, chip_ref, w_ref, out_ref, window, sem):
    total = w_ref.shape[1]
    wide = window.shape[2]
    width = total // 3
    copies, shifts = [], []
    for index in range(3 * head_count):
        kind, head = index // head_count, index % head_count
        start = kind * width + (chip_ref[0] * head_count + head) * HD
        base = jnp.minimum(start // LANE * LANE, total - wide)
        base = pl.multiple_of(base, LANE)
        shifts.append(start - base)
        copies.append(
            pltpu.make_async_copy(w_ref.at[:, pl.ds(base, wide)], window.at[index], sem.at[index])
        )
    for copy in copies:
        copy.start()
    for index, copy in enumerate(copies):
        copy.wait()
        rolled = pltpu.roll(window[index].astype(F32), wide - shifts[index], axis=1)[:, :LANE]
        inside = lax.broadcasted_iota(jnp.int32, rolled.shape, 1) < HD
        out_ref[:, index * LANE : (index + 1) * LANE] = jnp.where(inside, rolled, 0.0).astype(BF16)


def chip_weights(chip, w_qkv, head_count):
    depth = w_qkv.shape[0]
    wide = 2 * LANE
    return pl.pallas_call(
        functools.partial(weight_kernel, head_count),
        in_specs=[smem(), hbm()],
        out_specs=vmem(),
        out_shape=jax.ShapeDtypeStruct((depth, 3 * head_count * LANE), BF16),
        scratch_shapes=[
            pltpu.VMEM((3 * head_count, depth, wide), BF16),
            pltpu.SemaphoreType.DMA((3 * head_count,)),
        ],
        name="chip_weights",
    )(chip, w_qkv)


def project_kernel(head_count, part_counts, *refs):
    w_ref, (q_ref, kv_ref) = refs[-3], refs[-2:]
    at, first_row = 0, 0
    for count in part_counts:
        rows = jnp.concatenate([ref[...] for ref in refs[at : at + count]], axis=0)
        at += count
        size = rows.shape[0]
        empty = rows[:, 0:1].astype(F32) > 0.5 * HUGE
        rows = jnp.where(empty, 0.0, rows.astype(F32)).astype(BF16)
        done = slice(first_row, first_row + size)
        first_row += size
        made = jnp.dot(rows, w_ref[...], preferred_element_type=F32)
        extra = lax.broadcasted_iota(jnp.int32, (size, LANE), 1) == HD
        for head in range(head_count):
            for kind in range(3):
                column = (kind * head_count + head) * LANE
                value = made[:, column : column + LANE]
                if kind == 0:
                    q_ref[head, done] = jnp.where(extra, 1.0, value).astype(BF16)
                elif kind == 1:
                    bias = jnp.where(empty, -HUGE, 0.0)
                    kv_ref[0, head, done] = jnp.where(extra, bias, value).astype(BF16)
                else:
                    kv_ref[1, head, done] = jnp.where(extra, 1.0, value).astype(BF16)


def project(chunks, weights, head_count):
    parts = [part for chunk in chunks for part in chunk]
    row_total = sum(part.shape[0] for part in parts)
    return pl.pallas_call(
        functools.partial(project_kernel, head_count, [len(chunk) for chunk in chunks]),
        in_specs=[vmem()] * (len(parts) + 1),
        out_specs=[vmem(), vmem()],
        out_shape=[
            jax.ShapeDtypeStruct((head_count, row_total, LANE), BF16),
            jax.ShapeDtypeStruct((2, head_count, row_total, LANE), BF16),
        ],
        name="project",
    )(*parts, weights)


def packed_rows(capacity, width):
    whole = width // LANE
    rest = width - whole * LANE
    if rest == 0:
        return whole * capacity, 0, 0
    if capacity % 16:
        return (whole + 1) * capacity, rest, capacity
    groups = LANE // rest
    tiles = -(-(capacity // 16) // groups)
    return whole * capacity + tiles * 16, rest, 16


def pack(block, write):
    capacity, width = block.shape
    whole = width // LANE
    for tile in range(whole):
        write(tile * capacity, block[:, tile * LANE : (tile + 1) * LANE])
    _, rest, size = packed_rows(capacity, width)
    if rest == 0:
        return
    tail = block[:, whole * LANE :]
    groups = 1 if size == capacity else LANE // rest
    for first in range(0, capacity // size, groups):
        pieces = [
            tail[group * size : (group + 1) * size]
            for group in range(first, min(first + groups, capacity // size))
        ]
        filler = LANE - rest * len(pieces)
        if filler:
            pieces.append(jnp.zeros((size, filler), block.dtype))
        write(whole * capacity + first // groups * size, jnp.concatenate(pieces, axis=1))


def unpack(packed, capacity, width):
    whole = width // LANE
    columns = [packed[tile * capacity : (tile + 1) * capacity] for tile in range(whole)]
    _, rest, size = packed_rows(capacity, width)
    if rest:
        groups = 1 if size == capacity else LANE // rest
        pieces = []
        for group in range(capacity // size):
            top = whole * capacity + group // groups * size
            left = group % groups * rest
            pieces.append(packed[top : top + size, left : left + rest])
        columns.append(jnp.concatenate(pieces, axis=0))
    return jnp.concatenate(columns, axis=1)


def attend_kernel(chips, capacity, target_ref, q_ref, kv_ref, other_ref, out_ref):
    head_count = q_ref.shape[0]
    factor = math.log2(math.e) / math.sqrt(HD)
    nt = (((1,), (1,)), ((), ()))
    results = []
    for head in range(head_count):
        query = q_ref[head]
        scores = [
            lax.dot_general(query, ref[0, head], nt, preferred_element_type=F32)
            for ref in (kv_ref, other_ref)
        ]
        top = jnp.maximum(*[jnp.max(score, axis=1, keepdims=True) for score in scores])
        mixed = None
        for score, ref in zip(scores, (kv_ref, other_ref)):
            probs = jnp.exp2((score - top) * factor).astype(BF16)
            term = jnp.dot(probs, ref[1, head], preferred_element_type=F32)
            mixed = term if mixed is None else mixed + term
        results.append(mixed[:, :HD] / mixed[:, HD : HD + 1])
    rows = jnp.concatenate(results, axis=1).astype(BF16)
    for chip in range(chips):
        block = rows[chip * capacity : (chip + 1) * capacity]
        across, along = target_ref[1 + 2 * chip], target_ref[2 + 2 * chip]

        def write(first, value):
            out_ref[across, 0, along, first : first + value.shape[0]] = value

        pack(block, write)


def attend(targets, queries, kv, other, across, bags, along, capacity):
    head_count, row_total, _ = queries.shape
    chunk_rows = across * along * capacity
    out_rows = packed_rows(capacity, head_count * HD)[0]
    grid_spec = pltpu.PrefetchScalarGridSpec(
        num_scalar_prefetch=1,
        grid=(bags,),
        in_specs=[
            pl.BlockSpec((head_count, chunk_rows, LANE), lambda k, t: (0, k, 0)),
            pl.BlockSpec(kv.shape, lambda k, t: (0, 0, 0, 0), pipeline_mode=pl.Buffered(1)),
            pl.BlockSpec(other.shape, lambda k, t: (0, 0, 0, 0), pipeline_mode=pl.Buffered(1)),
        ],
        out_specs=pl.BlockSpec((across, 1, along, out_rows, LANE), lambda k, t: (0, t[0] ^ k, 0, 0, 0)),
    )
    return pl.pallas_call(
        functools.partial(attend_kernel, across * along, capacity),
        grid_spec=grid_spec,
        out_shape=jax.ShapeDtypeStruct((across, bags, along, out_rows, LANE), BF16),
        name="attend",
    )(targets, queries, kv, other)


def finish_kernel(
    capacity, tokens_ref, seq_ref, mod_ref, mixed_ref, w_out, w_fc1, w_fc2, out_ref, v_out, v_fc1, v_fc2, sems
):
    copies = [
        pltpu.make_async_copy(source, target, sems.at[index])
        for index, (source, target) in enumerate(((w_out, v_out), (w_fc1, v_fc1), (w_fc2, v_fc2)))
    ]
    for copy in copies:
        copy.start()
    across, bags, along, _, _ = mixed_ref.shape
    row_count, width = tokens_ref.shape
    seq_row = seq_ref[...].astype(F32)
    position = slot_of_row(jnp.floor(seq_row / SEQ_BAG), capacity)
    slot_ids = lax.broadcasted_iota(jnp.int32, (bags * capacity, row_count), 0)
    pick = jnp.where(slot_ids == position, 1.0, 0.0).astype(BF16)
    seq_column = to_column(seq_row)
    chip_width = width // (across * along)
    slots = jnp.concatenate(
        [
            jnp.concatenate(
                [
                    unpack(mixed_ref[x, bag, y], capacity, chip_width)
                    for x in range(across)
                    for y in range(along)
                ],
                axis=1,
            )
            for bag in range(bags)
        ],
        axis=0,
    )
    tn = (((0,), (0,)), ((), ()))
    attended = lax.dot_general(pick, slots, tn, preferred_element_type=F32).astype(BF16)

    def per_row(column):
        value = jnp.broadcast_to(mod_ref[0, column : column + 1], (row_count, width))
        for seq in range(1, mod_ref.shape[0]):
            value = jnp.where(seq_column == seq, mod_ref[seq, column : column + 1], value)
        return value

    copies[0].wait()
    branch = jnp.dot(attended, v_out[...], preferred_element_type=F32)
    hidden = (tokens_ref[...].astype(F32) + per_row(2) * branch).astype(BF16)
    normed = (layer_norm(hidden.astype(F32)) * (1.0 + per_row(4)) + per_row(3)).astype(BF16)
    copies[1].wait()
    active = jax.nn.gelu(jnp.dot(normed, v_fc1[...], preferred_element_type=F32), approximate=True)
    active = active.astype(BF16)
    copies[2].wait()
    last = jnp.dot(active, v_fc2[...], preferred_element_type=F32)
    out_ref[...] = (hidden.astype(F32) + per_row(5) * last).astype(BF16)


def finish(tokens, seq_row, modulation, mixed, w_out, w_fc1, w_fc2, capacity):
    return pl.pallas_call(
        functools.partial(finish_kernel, capacity),
        in_specs=[vmem(), vmem(), vmem(), vmem(), hbm(), hbm(), hbm()],
        out_specs=vmem(),
        out_shape=jax.ShapeDtypeStruct(tokens.shape, BF16),
        scratch_shapes=[
            pltpu.VMEM(w_out.shape, BF16),
            pltpu.VMEM(w_fc1.shape, BF16),
            pltpu.VMEM(w_fc2.shape, BF16),
            pltpu.SemaphoreType.DMA((3,)),
        ],
        name="finish",
    )(tokens, seq_row, modulation, mixed, w_out, w_fc1, w_fc2)


def shards(tokens, row_seq, modulation, w_qkv, w_out, w_fc1, w_fc2):
    bags, sp = lax.axis_size("bag"), lax.axis_size("sp")
    along, across, cores = sp // bags, bags // 2, 2
    chips = across * along
    row_count, width = tokens.shape
    capacity = row_count // bags * 5 // 4
    head_count = width // HD // chips
    my_bag, my_sp = lax.axis_index("bag"), lax.axis_index("sp")
    my_x, my_z, my_y = my_bag // cores, my_sp // along, my_sp % along

    def swap(value, dx=0, core=0, dz=0, dy=0):
        pairs = []
        for b in range(bags):
            for s in range(sp):
                b2 = ((b // cores) ^ dx) * cores + ((b % cores) ^ core)
                s2 = ((s // along) ^ dz) * along + ((s % along) ^ dy)
                pairs.append((b * sp + s, b2 * sp + s2))
        return lax.ppermute(value, AXES, pairs)

    seq_row = row_seq.reshape(1, row_count)
    place = my_z.reshape(1).astype(jnp.int32)
    blocks = slot_rows(place, tokens, seq_row, modulation, bags, capacity)
    weights = chip_weights((my_x * along + my_y).reshape(1).astype(jnp.int32), w_qkv, head_count)
    blocks = [block if k == 0 else swap(block, dz=k) for k, block in enumerate(blocks)]
    chunks = []
    half = -(-capacity // 32) * 16
    for block in blocks:
        if across == 2 and along == 2:
            from_x, from_y = swap(block, dx=1), swap(block, dy=1)
            upper, lower = swap(from_x[:half], dy=1), swap(from_y[half:], dx=1)
            chunks.append([block, from_y, from_x, upper, lower])
        else:
            chunks.append(
                [
                    swap(block, dx=j // along, dy=j % along) if j else block
                    for j in range(chips)
                ]
            )
    queries, kv = project(chunks, weights, head_count)
    other = swap(kv, core=1)
    targets = [my_z]
    for j in range(chips):
        targets += [my_x ^ (j // along), my_y ^ (j % along)]
    mixed = attend(jnp.stack(targets).astype(jnp.int32), queries, kv, other, across, bags, along, capacity)
    groups = [
        [(x * cores + core) * sp + s for x in range(across) for s in range(sp)] for core in range(cores)
    ]
    shape = mixed.shape
    mixed = lax.all_to_all(
        mixed.reshape((across * sp,) + shape[3:]), AXES, 0, 0, axis_index_groups=groups, tiled=True
    ).reshape(shape)
    return finish(tokens, seq_row, modulation, mixed, w_out, w_fc1, w_fc2, capacity)


def solution(mesh):
    placed = (P(("bag", "sp"), None), P(("bag", "sp")), P(), P(), P(), P(), P())
    return jax.shard_map(
        shards, mesh=mesh, in_specs=placed, out_specs=P(("bag", "sp"), None), check_vma=False
    )
```

```python
import functools
import math

import jax
import jax.numpy as jnp
from jax import lax
from jax.experimental import pallas as pl
from jax.experimental.pallas import tpu as pltpu
from jax.sharding import PartitionSpec as P


HD = 72
SEQ_BAG = 1
LANE = 128
EPS = 1e-06
HUGE = 1e30
AXES = ("bag", "sp")
BF16, F32 = jnp.bfloat16, jnp.float32


def vmem():
    return pl.BlockSpec(memory_space=pltpu.VMEM)


def smem():
    return pl.BlockSpec(memory_space=pltpu.SMEM)


def hbm():
    return pl.BlockSpec(memory_space=pl.ANY)


def layer_norm(values):
    center = values - jnp.mean(values, axis=-1, keepdims=True)
    spread = jnp.mean(center * center, axis=-1, keepdims=True)
    return center * lax.rsqrt(spread + EPS)


def to_column(row):
    n = row.shape[1]
    diagonal = lax.broadcasted_iota(jnp.int32, (n, n), 0) == lax.broadcasted_iota(jnp.int32, (n, n), 1)
    return jnp.sum(jnp.where(diagonal, jnp.broadcast_to(row, (n, n)), 0.0), axis=1, keepdims=True)


def slot_of_row(bag_row, capacity):
    n = bag_row.shape[1]
    earlier = lax.broadcasted_iota(jnp.int32, (n, n), 0) < lax.broadcasted_iota(jnp.int32, (n, n), 1)
    same = jnp.broadcast_to(to_column(bag_row), (n, n)) == jnp.broadcast_to(bag_row, (n, n))
    rank = jnp.sum(jnp.where(same & earlier, 1.0, 0.0), axis=0, keepdims=True)
    return (bag_row * capacity + rank).astype(jnp.int32)


def slot_kernel(capacity, place_ref, tokens_ref, seq_ref, mod_ref, *out_refs):
    me = place_ref[0]
    row_count, width = tokens_ref.shape
    block_count = len(out_refs)
    bag_row = ((seq_ref[...] // SEQ_BAG) ^ me).astype(F32)
    position = slot_of_row(bag_row, capacity)
    slot_ids = lax.broadcasted_iota(jnp.int32, (block_count * capacity, row_count), 0)
    pick = jnp.where(slot_ids == position, 1.0, 0.0)
    filled = jnp.sum(pick, axis=1, keepdims=True)
    rows = jnp.dot(pick.astype(BF16), tokens_ref[...], preferred_element_type=F32)
    first = lax.broadcasted_iota(jnp.int32, (capacity, width), 1) == 0
    for block, out_ref in enumerate(out_refs):
        part = slice(block * capacity, (block + 1) * capacity)
        mods = mod_ref[block ^ me]
        normed = layer_norm(rows[part]) * (1.0 + mods[1:2]) + mods[0:1]
        normed = jnp.where(first & (filled[part] < 0.5), HUGE, normed)
        out_ref[...] = normed.astype(BF16)


def slot_rows(place, tokens, seq_row, modulation, bag_count, capacity):
    width = tokens.shape[1]
    return pl.pallas_call(
        functools.partial(slot_kernel, capacity),
        in_specs=[smem(), vmem(), vmem(), vmem()],
        out_specs=[vmem()] * bag_count,
        out_shape=[jax.ShapeDtypeStruct((capacity, width), BF16)] * bag_count,
        name="slot_rows",
    )(place, tokens, seq_row, modulation)


def weight_kernel(part, chip_ref, w_ref, out_ref, window, sem):
    total = w_ref.shape[1]
    wide = window.shape[2]
    copies, shifts = [], []
    for kind in range(3):
        start = kind * (total // 3) + chip_ref[0] * part
        base = pl.multiple_of(jnp.minimum(start // LANE * LANE, total - wide), LANE)
        shifts.append(start - base)
        copies.append(
            pltpu.make_async_copy(w_ref.at[:, pl.ds(base, wide)], window.at[kind], sem.at[kind])
        )
    for copy in copies:
        copy.start()
    pieces = []
    for kind, copy in enumerate(copies):
        copy.wait()
        rolled = pltpu.roll(window[kind].astype(F32), wide - shifts[kind], axis=1)
        pieces.append(rolled[:, :part].astype(BF16))
    filler = out_ref.shape[1] - 3 * part
    if filler:
        pieces.append(jnp.zeros((w_ref.shape[0], filler), BF16))
    out_ref[...] = jnp.concatenate(pieces, axis=1)


def round_up(value, unit):
    return -(-value // unit) * unit


def chip_weights(chip, w_qkv, head_count):
    depth, part = w_qkv.shape[0], head_count * HD
    wide = round_up(part + LANE - math.gcd(part, LANE), LANE)
    return pl.pallas_call(
        functools.partial(weight_kernel, part),
        in_specs=[smem(), hbm()],
        out_specs=vmem(),
        out_shape=jax.ShapeDtypeStruct((depth, round_up(3 * part, LANE)), BF16),
        scratch_shapes=[pltpu.VMEM((3, depth, wide), BF16), pltpu.SemaphoreType.DMA((3,))],
        cost_estimate=pl.CostEstimate(flops=10**9, bytes_accessed=10**7, transcendentals=0),
        name="chip_weights",
    )(chip, w_qkv)


def project_kernel(head_count, *refs):
    w_ref, (q_ref, kv_ref) = refs[-3], refs[-2:]
    rows = jnp.concatenate([ref[...] for ref in refs[:-3]], axis=0)
    size = rows.shape[0]
    factor = math.log2(math.e) / math.sqrt(HD)
    empty = rows[:, :1].astype(F32) > 0.5 * HUGE
    start = jnp.where(empty, 0.0, rows[:, :LANE].astype(F32)).astype(BF16)
    rows = jnp.concatenate([start, rows[:, LANE:]], axis=1)
    made = jnp.dot(rows, w_ref[...], preferred_element_type=F32)
    lane = lax.broadcasted_iota(jnp.int32, (size, LANE), 1)
    bias = jnp.where(empty, -HUGE, 0.0)
    for kind in range(3):
        for head in range(head_count):
            column = (kind * head_count + head) * HD
            base, shift = column // LANE * LANE, column % LANE
            wide = LANE if shift + HD <= LANE else 2 * LANE
            value = made[:, base : base + wide]
            if shift:
                value = pltpu.roll(value, wide - shift, axis=1)
            value = value[:, :LANE]
            if kind == 0:
                value, beside = value * factor, 1.0
            else:
                beside = bias if kind == 1 else 1.0
            value = jnp.where(lane < HD, value, jnp.where(lane == HD, beside, 0.0)).astype(BF16)
            if kind == 0:
                q_ref[head] = value
            else:
                kv_ref[kind - 1, head] = value


def project(parts, weights, head_count):
    size, depth = sum(part.shape[0] for part in parts), weights.shape[0]
    return pl.pallas_call(
        functools.partial(project_kernel, head_count),
        in_specs=[vmem()] * (len(parts) + 1),
        out_specs=[vmem(), vmem()],
        out_shape=[
            jax.ShapeDtypeStruct((head_count, size, LANE), BF16),
            jax.ShapeDtypeStruct((2, head_count, size, LANE), BF16),
        ],
        cost_estimate=pl.CostEstimate(
            flops=2 * size * depth * weights.shape[1], bytes_accessed=4 * size * depth, transcendentals=0
        ),
        name="project",
    )(*parts, weights)


def packed_rows(capacity, width):
    whole = width // LANE
    rest = width - whole * LANE
    if rest == 0:
        return whole * capacity, 0, 0
    if capacity % 16:
        return (whole + 1) * capacity, rest, capacity
    groups = LANE // rest
    tiles = -(-(capacity // 16) // groups)
    return whole * capacity + tiles * 16, rest, 16


def pack(block, write):
    capacity, width = block.shape
    whole = width // LANE
    for tile in range(whole):
        write(tile * capacity, block[:, tile * LANE : (tile + 1) * LANE])
    _, rest, size = packed_rows(capacity, width)
    if rest == 0:
        return
    tail = block[:, whole * LANE :]
    groups = 1 if size == capacity else LANE // rest
    for first in range(0, capacity // size, groups):
        pieces = [
            tail[group * size : (group + 1) * size]
            for group in range(first, min(first + groups, capacity // size))
        ]
        filler = LANE - rest * len(pieces)
        if filler:
            pieces.append(jnp.zeros((size, filler), block.dtype))
        write(whole * capacity + first // groups * size, jnp.concatenate(pieces, axis=1))


def unpack(packed, capacity, width):
    whole = width // LANE
    columns = [packed[tile * capacity : (tile + 1) * capacity] for tile in range(whole)]
    _, rest, size = packed_rows(capacity, width)
    if rest:
        groups = 1 if size == capacity else LANE // rest
        pieces = []
        for group in range(capacity // size):
            top = whole * capacity + group // groups * size
            left = group % groups * rest
            pieces.append(packed[top : top + size, left : left + rest])
        columns.append(jnp.concatenate(pieces, axis=0))
    return jnp.concatenate(columns, axis=1)


def attend_kernel(chips, capacity, piece_count, *refs):
    q_ref, pieces, out_ref = refs[0], refs[1 : 1 + piece_count], refs[1 + piece_count]
    if piece_count > 1:
        kv_ref = refs[2 + piece_count]
        at = 0
        for ref in pieces:
            kv_ref[:, :, at : at + ref.shape[2]] = ref[...]
            at += ref.shape[2]
    else:
        kv_ref = pieces[0]
    nt = (((1,), (1,)), ((), ()))
    results = []
    for head in range(q_ref.shape[0]):
        score = lax.dot_general(q_ref[head], kv_ref[0, head], nt, preferred_element_type=F32)
        top = jnp.max(score, axis=1, keepdims=True)
        probs = jnp.exp2(score - top).astype(BF16)
        mixed = jnp.dot(probs, kv_ref[1, head], preferred_element_type=F32)
        results.append(mixed[:, :HD] / mixed[:, HD : HD + 1])
    rows = jnp.concatenate(results, axis=1).astype(BF16)
    for chip in range(chips):
        block = rows[chip * capacity : (chip + 1) * capacity]

        def write(first, value):
            out_ref[chip, first : first + value.shape[0]] = value

        pack(block, write)


def attend(queries, pieces, chips, capacity):
    head_count = queries.shape[0]
    keys = sum(piece.shape[2] for piece in pieces)
    out_rows = packed_rows(capacity, head_count * HD)[0]
    out_shape = [jax.ShapeDtypeStruct((chips, out_rows, LANE), BF16)]
    if len(pieces) > 1:
        out_shape.append(jax.ShapeDtypeStruct((2, head_count, keys, LANE), BF16))
    made = pl.pallas_call(
        functools.partial(attend_kernel, chips, capacity, len(pieces)),
        in_specs=[vmem()] * (1 + len(pieces)),
        out_specs=[vmem()] * len(out_shape),
        out_shape=out_shape,
        cost_estimate=pl.CostEstimate(
            flops=4 * head_count * queries.shape[1] * keys * LANE,
            bytes_accessed=4 * head_count * keys * LANE,
            transcendentals=head_count * queries.shape[1] * keys,
        ),
        name="attend",
    )(queries, *pieces)
    return made[0], (made[1] if len(pieces) > 1 else pieces[0])


def finish_kernel(capacity, chips, place_ref, tokens_ref, seq_ref, mod_ref, w_out, w_fc1, w_fc2, *refs):
    parts, out_ref, whole = refs[:chips], refs[chips], refs[chips + 1]
    row_count, width = tokens_ref.shape
    for index, part in enumerate(parts):
        whole[place_ref[1] ^ index] = part[...]
    bags = parts[0].shape[0]
    seq_row = seq_ref[...]
    position = slot_of_row(((seq_row // SEQ_BAG) ^ place_ref[0]).astype(F32), capacity)
    slot_ids = lax.broadcasted_iota(jnp.int32, (bags * capacity, row_count), 0)
    pick = jnp.where(slot_ids == position, 1.0, 0.0).astype(BF16)
    seq_column = to_column(seq_row.astype(F32))
    slots = jnp.concatenate(
        [
            jnp.concatenate(
                [unpack(whole[chip, bag], capacity, width // chips) for chip in range(chips)], axis=1
            )
            for bag in range(bags)
        ],
        axis=0,
    )
    tn = (((0,), (0,)), ((), ()))
    attended = lax.dot_general(pick, slots, tn, preferred_element_type=F32).astype(BF16)

    def per_row(column):
        value = jnp.broadcast_to(mod_ref[0, column : column + 1], (row_count, width))
        for seq in range(1, mod_ref.shape[0]):
            value = jnp.where(seq_column == seq, mod_ref[seq, column : column + 1], value)
        return value

    branch = jnp.dot(attended, w_out[...], preferred_element_type=F32)
    hidden = (tokens_ref[...].astype(F32) + per_row(2) * branch).astype(BF16)
    normed = (layer_norm(hidden.astype(F32)) * (1.0 + per_row(4)) + per_row(3)).astype(BF16)
    active = jax.nn.gelu(jnp.dot(normed, w_fc1[...], preferred_element_type=F32), approximate=True)
    last = jnp.dot(active.astype(BF16), w_fc2[...], preferred_element_type=F32)
    out_ref[...] = (hidden.astype(F32) + per_row(5) * last).astype(BF16)


def finish(place, tokens, seq_row, modulation, parts, w_out, w_fc1, w_fc2, capacity):
    chips = len(parts)
    return pl.pallas_call(
        functools.partial(finish_kernel, capacity, chips),
        in_specs=[smem()] + [vmem()] * (6 + chips),
        out_specs=vmem(),
        out_shape=jax.ShapeDtypeStruct(tokens.shape, BF16),
        scratch_shapes=[pltpu.VMEM((chips,) + parts[0].shape, BF16)],
        name="finish",
    )(place, tokens, seq_row, modulation, w_out, w_fc1, w_fc2, *parts)


def layer(tokens, row_seq, modulation, w_qkv, w_out, w_fc1, w_fc2):
    bags, sp = lax.axis_size("bag"), lax.axis_size("sp")
    along, across, cores = sp // bags, bags // 2, 2
    chips = across * along
    row_count, width = tokens.shape
    capacity = row_count // bags * 5 // 4
    head_count = width // HD // chips
    my_bag, my_sp = lax.axis_index("bag"), lax.axis_index("sp")
    my_x, my_z, my_y = my_bag // cores, my_sp // along, my_sp % along

    def swap(value, dx=0, core=0, dz=0, dy=0):
        pairs = []
        for b in range(bags):
            for s in range(sp):
                b2 = ((b // cores) ^ dx) * cores + ((b % cores) ^ core)
                s2 = ((s // along) ^ dz) * along + ((s % along) ^ dy)
                pairs.append((b * sp + s, b2 * sp + s2))
        return lax.ppermute(value, AXES, pairs)

    seq_row = row_seq.reshape(1, row_count)
    place = jnp.stack([my_z, my_x * along + my_y]).astype(jnp.int32)
    blocks = slot_rows(place, tokens, seq_row, modulation, bags, capacity)
    weights = chip_weights(place[1:], w_qkv, head_count)
    blocks = [block if k == 0 else swap(block, dz=k) for k, block in enumerate(blocks)]
    half = round_up(capacity, 32) // 2
    queries, pieces = [], []
    for block in blocks:
        if across == 2 and along == 2:
            from_x, from_y = swap(block, dx=1), swap(block, dy=1)
            upper, lower = swap(from_x[:half], dy=1), swap(from_y[half:], dx=1)
            parts = [block, from_y, from_x, upper, lower]
        else:
            parts = [swap(block, dx=j // along, dy=j % along) if j else block for j in range(chips)]
        query, kv = project(parts, weights, head_count)
        queries.append(query)
        pieces += [kv, swap(kv, core=1)]
    mixed = [None] * bags
    for k in reversed(range(bags)):
        part, kv = attend(queries[k], pieces, chips, capacity)
        pieces = [kv]
        mixed[k] = swap(part, dz=k) if k else part
    shares = []
    for j in range(chips):
        share = jnp.stack([part[j] for part in mixed])
        shares.append(swap(share, dx=j // along, dy=j % along) if j else share)
    return finish(place, tokens, seq_row, modulation, shares, w_out, w_fc1, w_fc2, capacity)


def solution(mesh):
    placed = (P(("bag", "sp"), None), P(("bag", "sp")), P(), P(), P(), P(), P())
    return jax.shard_map(
        layer, mesh=mesh, in_specs=placed, out_specs=P(("bag", "sp"), None), check_vma=False
    )
```

```python
import functools
import math

import jax
import jax.numpy as jnp
from jax import lax
from jax.experimental import pallas as pl
from jax.experimental.pallas import tpu as pltpu
from jax.sharding import PartitionSpec as P


HD = 72
SEQ_BAG = 1
LANE = 128
EPS = 1e-06
HUGE = 1e30
AXES = ("bag", "sp")
BF16, F32 = jnp.bfloat16, jnp.float32


def vmem():
    return pl.BlockSpec(memory_space=pltpu.VMEM)


def hbm():
    return pl.BlockSpec(memory_space=pltpu.HBM)


def limit(mebibytes):
    return pltpu.CompilerParams(vmem_limit_bytes=mebibytes << 20)


def coordinates():
    along = lax.axis_size("sp") // lax.axis_size("bag")
    bag, sp = lax.axis_index("bag"), lax.axis_index("sp")
    return lax.div(sp, along), lax.div(bag, 2) * along + lax.rem(sp, along)


def layer_norm(values):
    center = values - jnp.mean(values, axis=-1, keepdims=True)
    spread = jnp.mean(center * center, axis=-1, keepdims=True)
    return center * lax.rsqrt(spread + EPS)


def to_column(row):
    n = row.shape[1]
    diagonal = lax.broadcasted_iota(jnp.int32, (n, n), 0) == lax.broadcasted_iota(jnp.int32, (n, n), 1)
    return jnp.sum(jnp.where(diagonal, jnp.broadcast_to(row, (n, n)), 0.0), axis=1, keepdims=True)


def slot_of_row(bag_row, capacity):
    n = bag_row.shape[1]
    earlier = lax.broadcasted_iota(jnp.int32, (n, n), 0) < lax.broadcasted_iota(jnp.int32, (n, n), 1)
    same = jnp.broadcast_to(to_column(bag_row), (n, n)) == jnp.broadcast_to(bag_row, (n, n))
    rank = jnp.sum(jnp.where(same & earlier, 1.0, 0.0), axis=0, keepdims=True)
    return (bag_row * capacity + rank).astype(jnp.int32)


def slot_kernel(capacity, tokens_ref, seq_ref, mod_ref, *out_refs):
    me, _ = coordinates()
    row_count, width = tokens_ref.shape
    block_count = len(out_refs)
    bag_row = ((seq_ref[...] // SEQ_BAG) ^ me).astype(F32)
    position = slot_of_row(bag_row, capacity)
    slot_ids = lax.broadcasted_iota(jnp.int32, (block_count * capacity, row_count), 0)
    pick = jnp.where(slot_ids == position, 1.0, 0.0)
    filled = jnp.sum(pick, axis=1, keepdims=True)
    rows = jnp.dot(pick.astype(BF16), tokens_ref[...], preferred_element_type=F32)
    first = lax.broadcasted_iota(jnp.int32, (capacity, width), 1) == 0
    for block, out_ref in enumerate(out_refs):
        part = slice(block * capacity, (block + 1) * capacity)
        shift, scale = [mod_ref[column, pl.ds(block ^ me, 1)] for column in (0, 1)]
        normed = layer_norm(rows[part]) * (1.0 + scale) + shift
        normed = jnp.where(first & (filled[part] < 0.5), HUGE, normed)
        out_ref[...] = normed.astype(BF16)


def slot_rows(tokens, seq_row, modulation, bag_count, capacity):
    width = tokens.shape[1]
    return pl.pallas_call(
        functools.partial(slot_kernel, capacity),
        in_specs=[vmem(), vmem(), vmem()],
        out_specs=[vmem()] * bag_count,
        out_shape=[jax.ShapeDtypeStruct((capacity, width), BF16)] * bag_count,
        compiler_params=limit(16),
        name="slot_rows",
    )(tokens, seq_row, modulation)


def weight_kernel(part, w_ref, out_ref, window, sem):
    total = w_ref.shape[1]
    wide = window.shape[2]
    copies, shifts = [], []
    _, chip = coordinates()
    for kind in range(3):
        start = kind * (total // 3) + chip * part
        base = pl.multiple_of(jnp.minimum(start // LANE * LANE, total - wide), LANE)
        shifts.append(start - base)
        copies.append(
            pltpu.make_async_copy(w_ref.at[:, pl.ds(base, wide)], window.at[kind], sem.at[kind])
        )
    for copy in copies:
        copy.start()
    pieces = []
    for kind, copy in enumerate(copies):
        copy.wait()
        rolled = pltpu.roll(window[kind].astype(F32), wide - shifts[kind], axis=1)
        pieces.append(rolled[:, :part].astype(BF16))
    filler = out_ref.shape[1] - 3 * part
    if filler:
        pieces.append(jnp.zeros((w_ref.shape[0], filler), BF16))
    out_ref[...] = jnp.concatenate(pieces, axis=1)


def round_up(value, unit):
    return -(-value // unit) * unit


def chip_weights(w_qkv, head_count):
    depth, part = w_qkv.shape[0], head_count * HD
    wide = round_up(part + LANE - math.gcd(part, LANE), LANE)
    return pl.pallas_call(
        functools.partial(weight_kernel, part),
        in_specs=[hbm()],
        out_specs=vmem(),
        out_shape=jax.ShapeDtypeStruct((depth, round_up(3 * part, LANE)), BF16),
        scratch_shapes=[pltpu.VMEM((3, depth, wide), BF16), pltpu.SemaphoreType.DMA((3,))],
        cost_estimate=pl.CostEstimate(flops=10**9, bytes_accessed=10**7, transcendentals=0),
        compiler_params=limit(20),
        name="chip_weights",
    )(w_qkv)


def project_kernel(head_count, *refs):
    w_ref, (q_ref, kv_ref) = refs[-3], refs[-2:]
    rows = jnp.concatenate([ref[...] for ref in refs[:-3]], axis=0)
    size = rows.shape[0]
    factor = math.log2(math.e) / math.sqrt(HD)
    empty = rows[:, :1].astype(F32) > 0.5 * HUGE
    start = jnp.where(empty, 0.0, rows[:, :LANE].astype(F32)).astype(BF16)
    rows = jnp.concatenate([start, rows[:, LANE:]], axis=1)
    made = jnp.dot(rows, w_ref[...], preferred_element_type=F32)
    lane = lax.broadcasted_iota(jnp.int32, (size, LANE), 1)
    bias = jnp.where(empty, -HUGE, 0.0)
    for kind in range(3):
        for head in range(head_count):
            column = (kind * head_count + head) * HD
            base, shift = column // LANE * LANE, column % LANE
            wide = LANE if shift + HD <= LANE else 2 * LANE
            value = made[:, base : base + wide]
            if shift:
                value = pltpu.roll(value, wide - shift, axis=1)
            value = value[:, :LANE]
            if kind == 0:
                value, beside = value * factor, 1.0
            else:
                beside = bias if kind == 1 else 1.0
            value = jnp.where(lane < HD, value, jnp.where(lane == HD, beside, 0.0)).astype(BF16)
            if kind == 0:
                q_ref[head] = value
            else:
                kv_ref[kind - 1, head] = value


def project(parts, weights, head_count):
    size, depth = sum(part.shape[0] for part in parts), weights.shape[0]
    return pl.pallas_call(
        functools.partial(project_kernel, head_count),
        in_specs=[vmem()] * (len(parts) + 1),
        out_specs=[vmem(), vmem()],
        out_shape=[
            jax.ShapeDtypeStruct((head_count, size, LANE), BF16),
            jax.ShapeDtypeStruct((2, head_count, size, LANE), BF16),
        ],
        cost_estimate=pl.CostEstimate(
            flops=2 * size * depth * weights.shape[1], bytes_accessed=4 * size * depth, transcendentals=0
        ),
        compiler_params=limit(12),
        name="project",
    )(*parts, weights)


def packed_rows(capacity, width):
    whole = width // LANE
    rest = width - whole * LANE
    if rest == 0:
        return whole * capacity, 0, 0
    if capacity % 16:
        return (whole + 1) * capacity, rest, capacity
    groups = LANE // rest
    tiles = -(-(capacity // 16) // groups)
    return whole * capacity + tiles * 16, rest, 16


def pack(block, write):
    capacity, width = block.shape
    whole = width // LANE
    for tile in range(whole):
        write(tile * capacity, block[:, tile * LANE : (tile + 1) * LANE])
    _, rest, size = packed_rows(capacity, width)
    if rest == 0:
        return
    tail = block[:, whole * LANE :]
    groups = 1 if size == capacity else LANE // rest
    for first in range(0, capacity // size, groups):
        pieces = [
            tail[group * size : (group + 1) * size]
            for group in range(first, min(first + groups, capacity // size))
        ]
        filler = LANE - rest * len(pieces)
        if filler:
            pieces.append(jnp.zeros((size, filler), block.dtype))
        write(whole * capacity + first // groups * size, jnp.concatenate(pieces, axis=1))


def unpack(packed, capacity, width):
    whole = width // LANE
    columns = [packed[tile * capacity : (tile + 1) * capacity] for tile in range(whole)]
    _, rest, size = packed_rows(capacity, width)
    if rest:
        groups = 1 if size == capacity else LANE // rest
        pieces = []
        for group in range(capacity // size):
            top = whole * capacity + group // groups * size
            left = group % groups * rest
            pieces.append(packed[top : top + size, left : left + rest])
        columns.append(jnp.concatenate(pieces, axis=0))
    return jnp.concatenate(columns, axis=1)


def attend_kernel(chips, capacity, piece_count, *refs):
    q_ref, pieces, out_ref = refs[0], refs[1 : 1 + piece_count], refs[1 + piece_count]
    if piece_count > 1:
        kv_ref = refs[2 + piece_count]
        at = 0
        for ref in pieces:
            kv_ref[:, :, at : at + ref.shape[2]] = ref[...]
            at += ref.shape[2]
    else:
        kv_ref = pieces[0]
    nt = (((1,), (1,)), ((), ()))
    results = []
    for head in range(q_ref.shape[0]):
        score = lax.dot_general(q_ref[head], kv_ref[0, head], nt, preferred_element_type=F32)
        top = jnp.max(score, axis=1, keepdims=True)
        probs = jnp.exp2(score - top).astype(BF16)
        mixed = jnp.dot(probs, kv_ref[1, head], preferred_element_type=F32)
        results.append(mixed[:, :HD] / mixed[:, HD : HD + 1])
    rows = jnp.concatenate(results, axis=1).astype(BF16)
    for chip in range(chips):
        block = rows[chip * capacity : (chip + 1) * capacity]

        def write(first, value):
            out_ref[chip, first : first + value.shape[0]] = value

        pack(block, write)


def attend(queries, pieces, chips, capacity):
    head_count = queries.shape[0]
    keys = sum(piece.shape[2] for piece in pieces)
    out_rows = packed_rows(capacity, head_count * HD)[0]
    out_shape = [jax.ShapeDtypeStruct((chips, out_rows, LANE), BF16)]
    if len(pieces) > 1:
        out_shape.append(jax.ShapeDtypeStruct((2, head_count, keys, LANE), BF16))
    made = pl.pallas_call(
        functools.partial(attend_kernel, chips, capacity, len(pieces)),
        in_specs=[vmem()] * (1 + len(pieces)),
        out_specs=[vmem()] * len(out_shape),
        out_shape=out_shape,
        cost_estimate=pl.CostEstimate(
            flops=4 * head_count * queries.shape[1] * keys * LANE,
            bytes_accessed=4 * head_count * keys * LANE,
            transcendentals=head_count * queries.shape[1] * keys,
        ),
        compiler_params=limit(24),
        name="attend",
    )(queries, *pieces)
    return made[0], (made[1] if len(pieces) > 1 else pieces[0])


def finish_kernel(capacity, chips, tokens_ref, seq_ref, mod_ref, w_out, w_fc1, w_fc2, *refs):
    parts, out_ref, whole = refs[:chips], refs[chips], refs[chips + 1]
    row_count, width = tokens_ref.shape
    plane, here = coordinates()
    for index, part in enumerate(parts):
        whole[here ^ index] = part[...]
    bags = parts[0].shape[0]
    seq_row = seq_ref[...]
    position = slot_of_row(((seq_row // SEQ_BAG) ^ plane).astype(F32), capacity)
    slot_ids = lax.broadcasted_iota(jnp.int32, (bags * capacity, row_count), 0)
    pick = jnp.where(slot_ids == position, 1.0, 0.0).astype(BF16)
    seq_column = to_column(seq_row.astype(F32))
    slots = jnp.concatenate(
        [
            jnp.concatenate(
                [unpack(whole[chip, bag], capacity, width // chips) for chip in range(chips)], axis=1
            )
            for bag in range(bags)
        ],
        axis=0,
    )
    tn = (((0,), (0,)), ((), ()))
    attended = lax.dot_general(pick, slots, tn, preferred_element_type=F32).astype(BF16)

    def per_row(column):
        value = jnp.broadcast_to(mod_ref[column, 0:1], (row_count, width))
        for seq in range(1, mod_ref.shape[1]):
            value = jnp.where(seq_column == seq, mod_ref[column, seq : seq + 1], value)
        return value

    branch = jnp.dot(attended, w_out[...], preferred_element_type=F32)
    hidden = (tokens_ref[...].astype(F32) + per_row(2) * branch).astype(BF16)
    normed = (layer_norm(hidden.astype(F32)) * (1.0 + per_row(4)) + per_row(3)).astype(BF16)
    active = jax.nn.gelu(jnp.dot(normed, w_fc1[...], preferred_element_type=F32), approximate=True)
    last = jnp.dot(active.astype(BF16), w_fc2[...], preferred_element_type=F32)
    out_ref[...] = (hidden.astype(F32) + per_row(5) * last).astype(BF16)


def finish(tokens, seq_row, modulation, parts, w_out, w_fc1, w_fc2, capacity):
    chips = len(parts)
    return pl.pallas_call(
        functools.partial(finish_kernel, capacity, chips),
        in_specs=[vmem()] * (6 + chips),
        out_specs=vmem(),
        out_shape=jax.ShapeDtypeStruct(tokens.shape, BF16),
        scratch_shapes=[pltpu.VMEM((chips,) + parts[0].shape, BF16)],
        compiler_params=limit(20),
        name="finish",
    )(tokens, seq_row, modulation, w_out, w_fc1, w_fc2, *parts)


def layer(tokens, row_seq, modulation, w_qkv, w_out, w_fc1, w_fc2):
    bags, sp = lax.axis_size("bag"), lax.axis_size("sp")
    along, across, cores = sp // bags, bags // 2, 2
    chips = across * along
    row_count, width = tokens.shape
    capacity = row_count // bags * 5 // 4
    head_count = width // HD // chips

    def swap(value, dx=0, core=0, dz=0, dy=0):
        pairs = []
        for b in range(bags):
            for s in range(sp):
                b2 = ((b // cores) ^ dx) * cores + ((b % cores) ^ core)
                s2 = ((s // along) ^ dz) * along + ((s % along) ^ dy)
                pairs.append((b * sp + s, b2 * sp + s2))
        return lax.ppermute(value, AXES, pairs)

    seq_row = row_seq.reshape(1, row_count)
    modulation = jnp.transpose(modulation, (1, 0, 2))
    blocks = slot_rows(tokens, seq_row, modulation, bags, capacity)
    weights = chip_weights(w_qkv, head_count)
    blocks = [block if k == 0 else swap(block, dz=k) for k, block in enumerate(blocks)]
    half = round_up(capacity, 32) // 2
    queries, pieces = [], []
    for block in blocks:
        if across == 2 and along == 2:
            from_x, from_y = swap(block, dx=1), swap(block, dy=1)
            upper, lower = swap(from_x[:half], dy=1), swap(from_y[half:], dx=1)
            parts = [block, from_y, from_x, upper, lower]
        else:
            parts = [swap(block, dx=j // along, dy=j % along) if j else block for j in range(chips)]
        query, kv = project(parts, weights, head_count)
        queries.append(query)
        pieces += [kv, swap(kv, core=1)]
    mixed = [None] * bags
    for k in reversed(range(bags)):
        part, kv = attend(queries[k], pieces, chips, capacity)
        pieces = [kv]
        mixed[k] = swap(part, dz=k) if k else part
    shares = []
    for j in range(chips):
        share = jnp.stack([part[j] for part in mixed])
        shares.append(swap(share, dx=j // along, dy=j % along) if j else share)
    return finish(tokens, seq_row, modulation, shares, w_out, w_fc1, w_fc2, capacity)


def solution(mesh):
    placed = (P(("bag", "sp"), None), P(("bag", "sp")), P(), P(), P(), P(), P())
    return jax.shard_map(
        layer, mesh=mesh, in_specs=placed, out_specs=P(("bag", "sp"), None), check_vma=False
    )
```

```python
import functools
import math

import jax
import jax.numpy as jnp
from jax import lax
from jax.experimental import pallas as pl
from jax.experimental.pallas import tpu as pltpu
from jax.sharding import PartitionSpec as P


HD = 72
SEQ_BAG = 1
LANE = 128
EPS = 1e-06
HUGE = 1e30
AXES = ("bag", "sp")
BF16, F32 = jnp.bfloat16, jnp.float32


def vmem():
    return pl.BlockSpec(memory_space=pltpu.VMEM)


def hbm():
    return pl.BlockSpec(memory_space=pltpu.HBM)


def limit(mebibytes):
    return pltpu.CompilerParams(vmem_limit_bytes=mebibytes << 20)


def coordinates():
    along = lax.axis_size("sp") // lax.axis_size("bag")
    bag, sp = lax.axis_index("bag"), lax.axis_index("sp")
    return lax.div(sp, along), lax.div(bag, 2) * along + lax.rem(sp, along)


def layer_norm(values):
    center = values - jnp.mean(values, axis=-1, keepdims=True)
    spread = jnp.mean(center * center, axis=-1, keepdims=True)
    return center * lax.rsqrt(spread + EPS)


def to_column(row):
    n = row.shape[1]
    diagonal = lax.broadcasted_iota(jnp.int32, (n, n), 0) == lax.broadcasted_iota(jnp.int32, (n, n), 1)
    return jnp.sum(jnp.where(diagonal, jnp.broadcast_to(row, (n, n)), 0.0), axis=1, keepdims=True)


def slot_of_row(bag_row, capacity):
    n = bag_row.shape[1]
    earlier = lax.broadcasted_iota(jnp.int32, (n, n), 0) < lax.broadcasted_iota(jnp.int32, (n, n), 1)
    same = jnp.broadcast_to(to_column(bag_row), (n, n)) == jnp.broadcast_to(bag_row, (n, n))
    rank = jnp.sum(jnp.where(same & earlier, 1.0, 0.0), axis=0, keepdims=True)
    return (bag_row * capacity + rank).astype(jnp.int32)


def slot_kernel(capacity, tokens_ref, seq_ref, mod_ref, *out_refs):
    me, _ = coordinates()
    row_count, width = tokens_ref.shape
    block_count = len(out_refs)
    bag_row = ((seq_ref[...] // SEQ_BAG) ^ me).astype(F32)
    position = slot_of_row(bag_row, capacity)
    slot_ids = lax.broadcasted_iota(jnp.int32, (block_count * capacity, row_count), 0)
    pick = jnp.where(slot_ids == position, 1.0, 0.0)
    filled = jnp.sum(pick, axis=1, keepdims=True)
    rows = jnp.dot(pick.astype(BF16), tokens_ref[...], preferred_element_type=F32)
    first = lax.broadcasted_iota(jnp.int32, (capacity, width), 1) == 0
    for block, out_ref in enumerate(out_refs):
        part = slice(block * capacity, (block + 1) * capacity)
        shift, scale = [mod_ref[column, pl.ds(block ^ me, 1)] for column in (0, 1)]
        normed = layer_norm(rows[part]) * (1.0 + scale) + shift
        normed = jnp.where(first & (filled[part] < 0.5), HUGE, normed)
        out_ref[...] = normed.astype(BF16)


def slot_rows(tokens, seq_row, modulation, bag_count, capacity):
    width = tokens.shape[1]
    return pl.pallas_call(
        functools.partial(slot_kernel, capacity),
        in_specs=[vmem(), vmem(), vmem()],
        out_specs=[vmem()] * bag_count,
        out_shape=[jax.ShapeDtypeStruct((capacity, width), BF16)] * bag_count,
        compiler_params=limit(16),
        name="slot_rows",
    )(tokens, seq_row, modulation)


def weight_kernel(part, w_ref, out_ref, window, sem):
    total = w_ref.shape[1]
    wide = window.shape[2]
    copies, shifts = [], []
    _, chip = coordinates()
    for kind in range(3):
        start = kind * (total // 3) + chip * part
        base = pl.multiple_of(jnp.minimum(start // LANE * LANE, total - wide), LANE)
        shifts.append(start - base)
        copies.append(
            pltpu.make_async_copy(w_ref.at[:, pl.ds(base, wide)], window.at[kind], sem.at[kind])
        )
    for copy in copies:
        copy.start()
    pieces = []
    for kind, copy in enumerate(copies):
        copy.wait()
        rolled = pltpu.roll(window[kind].astype(F32), wide - shifts[kind], axis=1)
        pieces.append(rolled[:, :part].astype(BF16))
    filler = out_ref.shape[1] - 3 * part
    if filler:
        pieces.append(jnp.zeros((w_ref.shape[0], filler), BF16))
    out_ref[...] = jnp.concatenate(pieces, axis=1)


def round_up(value, unit):
    return -(-value // unit) * unit


def chip_weights(w_qkv, head_count):
    depth, part = w_qkv.shape[0], head_count * HD
    wide = round_up(part + LANE - math.gcd(part, LANE), LANE)
    return pl.pallas_call(
        functools.partial(weight_kernel, part),
        in_specs=[hbm()],
        out_specs=vmem(),
        out_shape=jax.ShapeDtypeStruct((depth, round_up(3 * part, LANE)), BF16),
        scratch_shapes=[pltpu.VMEM((3, depth, wide), BF16), pltpu.SemaphoreType.DMA((3,))],
        cost_estimate=pl.CostEstimate(flops=10**9, bytes_accessed=10**7, transcendentals=0),
        compiler_params=limit(20),
        name="chip_weights",
    )(w_qkv)


def project_kernel(head_count, *refs):
    w_ref, (q_ref, kv_ref) = refs[-3], refs[-2:]
    rows = jnp.concatenate([ref[...] for ref in refs[:-3]], axis=0)
    size = rows.shape[0]
    factor = math.log2(math.e) / math.sqrt(HD)
    empty = rows[:, :1].astype(F32) > 0.5 * HUGE
    start = jnp.where(empty, 0.0, rows[:, :LANE].astype(F32)).astype(BF16)
    rows = jnp.concatenate([start, rows[:, LANE:]], axis=1)
    made = jnp.dot(rows, w_ref[...], preferred_element_type=F32)
    lane = lax.broadcasted_iota(jnp.int32, (size, LANE), 1)
    bias = jnp.where(empty, -HUGE, 0.0)
    for kind in range(3):
        for head in range(head_count):
            column = (kind * head_count + head) * HD
            base, shift = column // LANE * LANE, column % LANE
            wide = LANE if shift + HD <= LANE else 2 * LANE
            value = made[:, base : base + wide]
            if shift:
                value = pltpu.roll(value, wide - shift, axis=1)
            value = value[:, :LANE]
            if kind == 0:
                value, beside = value * factor, 1.0
            else:
                beside = bias if kind == 1 else 1.0
            value = jnp.where(lane < HD, value, jnp.where(lane == HD, beside, 0.0)).astype(BF16)
            if kind == 0:
                q_ref[head] = value
            else:
                kv_ref[kind - 1, head] = value


def project(parts, weights, head_count):
    size, depth = sum(part.shape[0] for part in parts), weights.shape[0]
    return pl.pallas_call(
        functools.partial(project_kernel, head_count),
        in_specs=[vmem()] * (len(parts) + 1),
        out_specs=[vmem(), vmem()],
        out_shape=[
            jax.ShapeDtypeStruct((head_count, size, LANE), BF16),
            jax.ShapeDtypeStruct((2, head_count, size, LANE), BF16),
        ],
        cost_estimate=pl.CostEstimate(
            flops=2 * size * depth * weights.shape[1], bytes_accessed=4 * size * depth, transcendentals=0
        ),
        compiler_params=limit(12),
        name="project",
    )(*parts, weights)


def packed_rows(capacity, width):
    whole = width // LANE
    rest = width - whole * LANE
    if rest == 0:
        return whole * capacity, 0, 0
    if capacity % 16:
        return (whole + 1) * capacity, rest, capacity
    groups = LANE // rest
    tiles = -(-(capacity // 16) // groups)
    return whole * capacity + tiles * 16, rest, 16


def pack(block, write):
    capacity, width = block.shape
    whole = width // LANE
    for tile in range(whole):
        write(tile * capacity, block[:, tile * LANE : (tile + 1) * LANE])
    _, rest, size = packed_rows(capacity, width)
    if rest == 0:
        return
    tail = block[:, whole * LANE :]
    groups = 1 if size == capacity else LANE // rest
    for first in range(0, capacity // size, groups):
        pieces = [
            tail[group * size : (group + 1) * size]
            for group in range(first, min(first + groups, capacity // size))
        ]
        filler = LANE - rest * len(pieces)
        if filler:
            pieces.append(jnp.zeros((size, filler), block.dtype))
        write(whole * capacity + first // groups * size, jnp.concatenate(pieces, axis=1))


def unpack(packed, capacity, width):
    whole = width // LANE
    columns = [packed[tile * capacity : (tile + 1) * capacity] for tile in range(whole)]
    _, rest, size = packed_rows(capacity, width)
    if rest:
        groups = 1 if size == capacity else LANE // rest
        pieces = []
        for group in range(capacity // size):
            top = whole * capacity + group // groups * size
            left = group % groups * rest
            pieces.append(packed[top : top + size, left : left + rest])
        columns.append(jnp.concatenate(pieces, axis=0))
    return jnp.concatenate(columns, axis=1)


def attend_kernel(chips, capacity, piece_count, *refs):
    q_ref, pieces, out_ref = refs[0], refs[1 : 1 + piece_count], refs[1 + piece_count]
    if piece_count > 1:
        kv_ref = refs[2 + piece_count]
        at = 0
        for ref in pieces:
            kv_ref[:, :, at : at + ref.shape[2]] = ref[...]
            at += ref.shape[2]
    else:
        kv_ref = pieces[0]
    nt = (((1,), (1,)), ((), ()))
    results = []
    for head in range(q_ref.shape[0]):
        score = lax.dot_general(q_ref[head], kv_ref[0, head], nt, preferred_element_type=F32)
        top = jnp.max(score, axis=1, keepdims=True)
        probs = jnp.exp2(score - top).astype(BF16)
        mixed = jnp.dot(probs, kv_ref[1, head], preferred_element_type=F32)
        results.append(mixed[:, :HD] / mixed[:, HD : HD + 1])
    rows = jnp.concatenate(results, axis=1).astype(BF16)
    for chip in range(chips):
        block = rows[chip * capacity : (chip + 1) * capacity]

        def write(first, value):
            out_ref[chip, first : first + value.shape[0]] = value

        pack(block, write)


def attend(queries, pieces, chips, capacity):
    head_count = queries.shape[0]
    keys = sum(piece.shape[2] for piece in pieces)
    out_rows = packed_rows(capacity, head_count * HD)[0]
    out_shape = [jax.ShapeDtypeStruct((chips, out_rows, LANE), BF16)]
    if len(pieces) > 1:
        out_shape.append(jax.ShapeDtypeStruct((2, head_count, keys, LANE), BF16))
    made = pl.pallas_call(
        functools.partial(attend_kernel, chips, capacity, len(pieces)),
        in_specs=[vmem()] * (1 + len(pieces)),
        out_specs=[vmem()] * len(out_shape),
        out_shape=out_shape,
        cost_estimate=pl.CostEstimate(
            flops=4 * head_count * queries.shape[1] * keys * LANE,
            bytes_accessed=4 * head_count * keys * LANE,
            transcendentals=head_count * queries.shape[1] * keys,
        ),
        compiler_params=limit(24),
        name="attend",
    )(queries, *pieces)
    return made[0], (made[1] if len(pieces) > 1 else pieces[0])


def finish_kernel(capacity, chips, rounds, tokens_ref, seq_ref, mod_ref, w_out, w_fc1, w_fc2, *refs):
    parts, out_ref, whole = refs[:-2], refs[-2], refs[-1]
    row_count, width = tokens_ref.shape
    plane, here = coordinates()
    for index, part in enumerate(parts):
        for at, bag in enumerate(rounds[index // chips]):
            whole[here ^ (index % chips), bag] = part[at]
    bags = whole.shape[1]
    seq_row = seq_ref[...]
    position = slot_of_row(((seq_row // SEQ_BAG) ^ plane).astype(F32), capacity)
    slot_ids = lax.broadcasted_iota(jnp.int32, (bags * capacity, row_count), 0)
    pick = jnp.where(slot_ids == position, 1.0, 0.0).astype(BF16)
    seq_column = to_column(seq_row.astype(F32))
    slots = jnp.concatenate(
        [
            jnp.concatenate(
                [unpack(whole[chip, bag], capacity, width // chips) for chip in range(chips)], axis=1
            )
            for bag in range(bags)
        ],
        axis=0,
    )
    tn = (((0,), (0,)), ((), ()))
    attended = lax.dot_general(pick, slots, tn, preferred_element_type=F32).astype(BF16)

    def per_row(column):
        value = jnp.broadcast_to(mod_ref[column, 0:1], (row_count, width))
        for seq in range(1, mod_ref.shape[1]):
            value = jnp.where(seq_column == seq, mod_ref[column, seq : seq + 1], value)
        return value

    branch = jnp.dot(attended, w_out[...], preferred_element_type=F32)
    hidden = (tokens_ref[...].astype(F32) + per_row(2) * branch).astype(BF16)
    normed = (layer_norm(hidden.astype(F32)) * (1.0 + per_row(4)) + per_row(3)).astype(BF16)
    active = jax.nn.gelu(jnp.dot(normed, w_fc1[...], preferred_element_type=F32), approximate=True)
    last = jnp.dot(active.astype(BF16), w_fc2[...], preferred_element_type=F32)
    out_ref[...] = (hidden.astype(F32) + per_row(5) * last).astype(BF16)


def finish(tokens, seq_row, modulation, parts, rounds, w_out, w_fc1, w_fc2, capacity, chips):
    bags = sum(len(members) for members in rounds)
    return pl.pallas_call(
        functools.partial(finish_kernel, capacity, chips, rounds),
        in_specs=[vmem()] * (6 + len(parts)),
        out_specs=vmem(),
        out_shape=jax.ShapeDtypeStruct(tokens.shape, BF16),
        scratch_shapes=[pltpu.VMEM((chips, bags) + parts[0].shape[1:], BF16)],
        compiler_params=limit(20),
        name="finish",
    )(tokens, seq_row, modulation, w_out, w_fc1, w_fc2, *parts)


def layer(tokens, row_seq, modulation, w_qkv, w_out, w_fc1, w_fc2):
    bags, sp = lax.axis_size("bag"), lax.axis_size("sp")
    along, across, cores = sp // bags, bags // 2, 2
    chips = across * along
    row_count, width = tokens.shape
    capacity = row_count // bags * 5 // 4
    head_count = width // HD // chips

    def swap(value, dx=0, core=0, dz=0, dy=0):
        pairs = []
        for b in range(bags):
            for s in range(sp):
                b2 = ((b // cores) ^ dx) * cores + ((b % cores) ^ core)
                s2 = ((s // along) ^ dz) * along + ((s % along) ^ dy)
                pairs.append((b * sp + s, b2 * sp + s2))
        return lax.ppermute(value, AXES, pairs)

    seq_row = row_seq.reshape(1, row_count)
    modulation = jnp.transpose(modulation, (1, 0, 2))

    def in_place(value):
        return pltpu.with_memory_space_constraint(value, pltpu.HBM)

    blocks = slot_rows(in_place(tokens), in_place(seq_row), in_place(modulation), bags, capacity)
    weights = chip_weights(in_place(w_qkv), head_count)
    blocks = [block if k == 0 else swap(block, dz=k) for k, block in enumerate(blocks)]
    half = round_up(capacity, 32) // 2
    queries, pieces = [], []
    for block in blocks:
        if across == 2 and along == 2:
            from_x, from_y = swap(block, dx=1), swap(block, dy=1)
            upper, lower = swap(from_x[:half], dy=1), swap(from_y[half:], dx=1)
            parts = [block, from_y, from_x, upper, lower]
        else:
            parts = [swap(block, dx=j // along, dy=j % along) if j else block for j in range(chips)]
        query, kv = project(parts, weights, head_count)
        queries.append(query)
        pieces += [kv, swap(kv, core=1)]
    mixed = [None] * bags
    for k in reversed(range(bags)):
        part, kv = attend(queries[k], pieces, chips, capacity)
        pieces = [kv]
        mixed[k] = swap(part, dz=k) if k else part
    rounds = [[k for k in range(bags) if k != 2], [2]] if bags > 2 else [list(range(bags))]
    shares = []
    for members in rounds:
        for j in range(chips):
            share = jnp.stack([mixed[k][j] for k in members])
            shares.append(swap(share, dx=j // along, dy=j % along) if j else share)
    return finish(tokens, seq_row, modulation, shares, rounds, w_out, w_fc1, w_fc2, capacity, chips)


def solution(mesh):
    placed = (P(("bag", "sp"), None), P(("bag", "sp")), P(), P(), P(), P(), P())
    return jax.shard_map(
        layer, mesh=mesh, in_specs=placed, out_specs=P(("bag", "sp"), None), check_vma=False
    )
```

```python
import functools
import math

import jax
import jax.numpy as jnp
from jax import lax
from jax.experimental import pallas as pl
from jax.experimental.pallas import tpu as pltpu
from jax.sharding import PartitionSpec as P


HD = 72
SEQ_BAG = 1
LANE = 128
EPS = 1e-06
HUGE = 1e30
AXES = ("bag", "sp")
BF16, F32 = jnp.bfloat16, jnp.float32


def vmem():
    return pl.BlockSpec(memory_space=pltpu.VMEM)


def hbm():
    return pl.BlockSpec(memory_space=pltpu.HBM)


def limit(mebibytes):
    return pltpu.CompilerParams(vmem_limit_bytes=mebibytes << 20)


def coordinates():
    along = lax.axis_size("sp") // lax.axis_size("bag")
    bag, sp = lax.axis_index("bag"), lax.axis_index("sp")
    return lax.div(sp, along), lax.div(bag, 2) * along + lax.rem(sp, along)


def layer_norm(values):
    center = values - jnp.mean(values, axis=-1, keepdims=True)
    spread = jnp.mean(center * center, axis=-1, keepdims=True)
    return center * lax.rsqrt(spread + EPS)


def to_column(row):
    n = row.shape[1]
    diagonal = lax.broadcasted_iota(jnp.int32, (n, n), 0) == lax.broadcasted_iota(jnp.int32, (n, n), 1)
    return jnp.sum(jnp.where(diagonal, jnp.broadcast_to(row, (n, n)), 0.0), axis=1, keepdims=True)


def slot_of_row(bag_row, capacity):
    n = bag_row.shape[1]
    earlier = lax.broadcasted_iota(jnp.int32, (n, n), 0) < lax.broadcasted_iota(jnp.int32, (n, n), 1)
    same = jnp.broadcast_to(to_column(bag_row), (n, n)) == jnp.broadcast_to(bag_row, (n, n))
    rank = jnp.sum(jnp.where(same & earlier, 1.0, 0.0), axis=0, keepdims=True)
    return (bag_row * capacity + rank).astype(jnp.int32)


def slot_kernel(capacity, tokens_ref, seq_ref, mod_ref, *out_refs):
    me, _ = coordinates()
    row_count, width = tokens_ref.shape
    block_count = len(out_refs)
    bag_row = ((seq_ref[...] // SEQ_BAG) ^ me).astype(F32)
    position = slot_of_row(bag_row, capacity)
    slot_ids = lax.broadcasted_iota(jnp.int32, (block_count * capacity, row_count), 0)
    pick = jnp.where(slot_ids == position, 1.0, 0.0)
    filled = jnp.sum(pick, axis=1, keepdims=True)
    rows = jnp.dot(pick.astype(BF16), tokens_ref[...], preferred_element_type=F32)
    first = lax.broadcasted_iota(jnp.int32, (capacity, width), 1) == 0
    for block, out_ref in enumerate(out_refs):
        part = slice(block * capacity, (block + 1) * capacity)
        shift, scale = [mod_ref[column, pl.ds(block ^ me, 1)] for column in (0, 1)]
        normed = layer_norm(rows[part]) * (1.0 + scale) + shift
        normed = jnp.where(first & (filled[part] < 0.5), HUGE, normed)
        out_ref[...] = normed.astype(BF16)


def slot_rows(tokens, seq_row, modulation, bag_count, capacity):
    width = tokens.shape[1]
    return pl.pallas_call(
        functools.partial(slot_kernel, capacity),
        in_specs=[vmem(), vmem(), vmem()],
        out_specs=[vmem()] * bag_count,
        out_shape=[jax.ShapeDtypeStruct((capacity, width), BF16)] * bag_count,
        compiler_params=limit(16),
        name="slot_rows",
    )(tokens, seq_row, modulation)


def weight_kernel(part, w_ref, out_ref, window, sem):
    total = w_ref.shape[1]
    wide = window.shape[2]
    copies, shifts = [], []
    _, chip = coordinates()
    for kind in range(3):
        start = kind * (total // 3) + chip * part
        base = pl.multiple_of(jnp.minimum(start // LANE * LANE, total - wide), LANE)
        shifts.append(start - base)
        copies.append(
            pltpu.make_async_copy(w_ref.at[:, pl.ds(base, wide)], window.at[kind], sem.at[kind])
        )
    for copy in copies:
        copy.start()
    pieces = []
    for kind, copy in enumerate(copies):
        copy.wait()
        rolled = pltpu.roll(window[kind].astype(F32), wide - shifts[kind], axis=1)
        pieces.append(rolled[:, :part].astype(BF16))
    filler = out_ref.shape[1] - 3 * part
    if filler:
        pieces.append(jnp.zeros((w_ref.shape[0], filler), BF16))
    out_ref[...] = jnp.concatenate(pieces, axis=1)


def round_up(value, unit):
    return -(-value // unit) * unit


def chip_weights(w_qkv, head_count):
    depth, part = w_qkv.shape[0], head_count * HD
    wide = round_up(part + LANE - math.gcd(part, LANE), LANE)
    return pl.pallas_call(
        functools.partial(weight_kernel, part),
        in_specs=[hbm()],
        out_specs=vmem(),
        out_shape=jax.ShapeDtypeStruct((depth, round_up(3 * part, LANE)), BF16),
        scratch_shapes=[pltpu.VMEM((3, depth, wide), BF16), pltpu.SemaphoreType.DMA((3,))],
        cost_estimate=pl.CostEstimate(flops=10**9, bytes_accessed=10**7, transcendentals=0),
        compiler_params=limit(20),
        name="chip_weights",
    )(w_qkv)


def project_kernel(head_count, *refs):
    w_ref, (q_ref, kv_ref) = refs[-3], refs[-2:]
    rows = jnp.concatenate([ref[...] for ref in refs[:-3]], axis=0)
    size = rows.shape[0]
    factor = math.log2(math.e) / math.sqrt(HD)
    empty = rows[:, :1].astype(F32) > 0.5 * HUGE
    start = jnp.where(empty, 0.0, rows[:, :LANE].astype(F32)).astype(BF16)
    rows = jnp.concatenate([start, rows[:, LANE:]], axis=1)
    made = jnp.dot(rows, w_ref[...], preferred_element_type=F32)
    lane = lax.broadcasted_iota(jnp.int32, (size, LANE), 1)
    bias = jnp.where(empty, -HUGE, 0.0)
    for kind in range(3):
        for head in range(head_count):
            column = (kind * head_count + head) * HD
            base, shift = column // LANE * LANE, column % LANE
            wide = LANE if shift + HD <= LANE else 2 * LANE
            value = made[:, base : base + wide]
            if shift:
                value = pltpu.roll(value, wide - shift, axis=1)
            value = value[:, :LANE]
            if kind == 0:
                value, beside = value * factor, 1.0
            else:
                beside = bias if kind == 1 else 1.0
            value = jnp.where(lane < HD, value, jnp.where(lane == HD, beside, 0.0)).astype(BF16)
            if kind == 0:
                q_ref[head] = value
            else:
                kv_ref[kind - 1, head] = value


def project(parts, weights, head_count):
    size, depth = sum(part.shape[0] for part in parts), weights.shape[0]
    return pl.pallas_call(
        functools.partial(project_kernel, head_count),
        in_specs=[vmem()] * (len(parts) + 1),
        out_specs=[vmem(), vmem()],
        out_shape=[
            jax.ShapeDtypeStruct((head_count, size, LANE), BF16),
            jax.ShapeDtypeStruct((2, head_count, size, LANE), BF16),
        ],
        cost_estimate=pl.CostEstimate(
            flops=2 * size * depth * weights.shape[1], bytes_accessed=4 * size * depth, transcendentals=0
        ),
        compiler_params=limit(12),
        name="project",
    )(*parts, weights)


def packed_rows(capacity, width):
    whole = width // LANE
    rest = width - whole * LANE
    if rest == 0:
        return whole * capacity, 0, 0
    if capacity % 16:
        return (whole + 1) * capacity, rest, capacity
    groups = LANE // rest
    tiles = -(-(capacity // 16) // groups)
    return whole * capacity + tiles * 16, rest, 16


def pack(block, write):
    capacity, width = block.shape
    whole = width // LANE
    for tile in range(whole):
        write(tile * capacity, block[:, tile * LANE : (tile + 1) * LANE])
    _, rest, size = packed_rows(capacity, width)
    if rest == 0:
        return
    tail = block[:, whole * LANE :]
    groups = 1 if size == capacity else LANE // rest
    for first in range(0, capacity // size, groups):
        pieces = [
            tail[group * size : (group + 1) * size]
            for group in range(first, min(first + groups, capacity // size))
        ]
        filler = LANE - rest * len(pieces)
        if filler:
            pieces.append(jnp.zeros((size, filler), block.dtype))
        write(whole * capacity + first // groups * size, jnp.concatenate(pieces, axis=1))


def unpack(packed, capacity, width):
    whole = width // LANE
    columns = [packed[tile * capacity : (tile + 1) * capacity] for tile in range(whole)]
    _, rest, size = packed_rows(capacity, width)
    if rest:
        groups = 1 if size == capacity else LANE // rest
        pieces = []
        for group in range(capacity // size):
            top = whole * capacity + group // groups * size
            left = group % groups * rest
            pieces.append(packed[top : top + size, left : left + rest])
        columns.append(jnp.concatenate(pieces, axis=0))
    return jnp.concatenate(columns, axis=1)


def attend_kernel(chips, capacity, query_count, piece_count, *refs):
    queries, pieces = refs[:query_count], refs[query_count : query_count + piece_count]
    out_ref = refs[query_count + piece_count]
    if piece_count > 1:
        kv_ref = refs[-1]
        at = 0
        for ref in pieces:
            kv_ref[:, :, at : at + ref.shape[2]] = ref[...]
            at += ref.shape[2]
    else:
        kv_ref = pieces[0]
    nt = (((1,), (1,)), ((), ()))
    results = []
    for head in range(kv_ref.shape[1]):
        query = jnp.concatenate([ref[head] for ref in queries], axis=0)
        score = lax.dot_general(query, kv_ref[0, head], nt, preferred_element_type=F32)
        top = jnp.max(score, axis=1, keepdims=True)
        probs = jnp.exp2(score - top).astype(BF16)
        mixed = jnp.dot(probs, kv_ref[1, head], preferred_element_type=F32)
        results.append(mixed[:, :HD] / mixed[:, HD : HD + 1])
    rows = jnp.concatenate(results, axis=1).astype(BF16)
    for chip in range(chips):
        block = rows[chip * capacity : (chip + 1) * capacity]

        def write(first, value):
            out_ref[chip, first : first + value.shape[0]] = value

        pack(block, write)


def attend(queries, pieces, chips, capacity):
    head_count, rows = queries[0].shape[0], sum(query.shape[1] for query in queries)
    keys = sum(piece.shape[2] for piece in pieces)
    out_rows = packed_rows(capacity, head_count * HD)[0]
    out_shape = [jax.ShapeDtypeStruct((chips, out_rows, LANE), BF16)]
    if len(pieces) > 1:
        out_shape.append(jax.ShapeDtypeStruct((2, head_count, keys, LANE), BF16))
    made = pl.pallas_call(
        functools.partial(attend_kernel, chips, capacity, len(queries), len(pieces)),
        in_specs=[vmem()] * (len(queries) + len(pieces)),
        out_specs=[vmem()] * len(out_shape),
        out_shape=out_shape,
        cost_estimate=pl.CostEstimate(
            flops=4 * head_count * rows * keys * LANE,
            bytes_accessed=4 * head_count * keys * LANE,
            transcendentals=head_count * rows * keys,
        ),
        compiler_params=limit(24),
        name="attend",
    )(*queries, *pieces)
    return made[0], (made[1] if len(pieces) > 1 else pieces[0])


def finish_kernel(capacity, chips, rounds, tokens_ref, seq_ref, mod_ref, w_out, w_fc1, w_fc2, *refs):
    parts, out_ref, whole = refs[:-2], refs[-2], refs[-1]
    row_count, width = tokens_ref.shape
    plane, here = coordinates()
    for index, part in enumerate(parts):
        for at, bag in enumerate(rounds[index // chips]):
            whole[here ^ (index % chips), bag] = part[at]
    bags = whole.shape[1]
    seq_row = seq_ref[...]
    position = slot_of_row(((seq_row // SEQ_BAG) ^ plane).astype(F32), capacity)
    slot_ids = lax.broadcasted_iota(jnp.int32, (bags * capacity, row_count), 0)
    pick = jnp.where(slot_ids == position, 1.0, 0.0).astype(BF16)
    seq_column = to_column(seq_row.astype(F32))
    slots = jnp.concatenate(
        [
            jnp.concatenate(
                [unpack(whole[chip, bag], capacity, width // chips) for chip in range(chips)], axis=1
            )
            for bag in range(bags)
        ],
        axis=0,
    )
    tn = (((0,), (0,)), ((), ()))
    attended = lax.dot_general(pick, slots, tn, preferred_element_type=F32).astype(BF16)

    def per_row(column):
        value = jnp.broadcast_to(mod_ref[column, 0:1], (row_count, width))
        for seq in range(1, mod_ref.shape[1]):
            value = jnp.where(seq_column == seq, mod_ref[column, seq : seq + 1], value)
        return value

    branch = jnp.dot(attended, w_out[...], preferred_element_type=F32)
    hidden = (tokens_ref[...].astype(F32) + per_row(2) * branch).astype(BF16)
    normed = (layer_norm(hidden.astype(F32)) * (1.0 + per_row(4)) + per_row(3)).astype(BF16)
    active = jax.nn.gelu(jnp.dot(normed, w_fc1[...], preferred_element_type=F32), approximate=True)
    last = jnp.dot(active.astype(BF16), w_fc2[...], preferred_element_type=F32)
    out_ref[...] = (hidden.astype(F32) + per_row(5) * last).astype(BF16)


def finish(tokens, seq_row, modulation, parts, rounds, w_out, w_fc1, w_fc2, capacity, chips):
    bags = sum(len(members) for members in rounds)
    return pl.pallas_call(
        functools.partial(finish_kernel, capacity, chips, rounds),
        in_specs=[vmem()] * (6 + len(parts)),
        out_specs=vmem(),
        out_shape=jax.ShapeDtypeStruct(tokens.shape, BF16),
        scratch_shapes=[pltpu.VMEM((chips, bags) + parts[0].shape[1:], BF16)],
        compiler_params=limit(20),
        name="finish",
    )(tokens, seq_row, modulation, w_out, w_fc1, w_fc2, *parts)


def layer(tokens, row_seq, modulation, w_qkv, w_out, w_fc1, w_fc2):
    bags, sp = lax.axis_size("bag"), lax.axis_size("sp")
    along, across, cores = sp // bags, bags // 2, 2
    chips = across * along
    row_count, width = tokens.shape
    capacity = row_count // bags * 5 // 4
    head_count = width // HD // chips

    def swap(value, dx=0, core=0, dz=0, dy=0):
        pairs = []
        for b in range(bags):
            for s in range(sp):
                b2 = ((b // cores) ^ dx) * cores + ((b % cores) ^ core)
                s2 = ((s // along) ^ dz) * along + ((s % along) ^ dy)
                pairs.append((b * sp + s, b2 * sp + s2))
        return lax.ppermute(value, AXES, pairs)

    seq_row = row_seq.reshape(1, row_count)
    modulation = jnp.transpose(modulation, (1, 0, 2))

    def in_place(value):
        return pltpu.with_memory_space_constraint(value, pltpu.HBM)

    blocks = slot_rows(in_place(tokens), in_place(seq_row), in_place(modulation), bags, capacity)
    weights = chip_weights(in_place(w_qkv), head_count)
    blocks = [block if k == 0 else swap(block, dz=k) for k, block in enumerate(blocks)]
    half = round_up(capacity, 32) // 2
    queries, pieces = [], []
    for k, block in enumerate(blocks):
        if across == 2 and along == 2:
            from_x, from_y = swap(block, dx=1), swap(block, dy=1)
            upper, lower = swap(from_x[:half], dy=1), swap(from_y[half:], dx=1)
            parts = [block, from_y, from_x, upper, lower]
        else:
            parts = [swap(block, dx=j // along, dy=j % along) if j else block for j in range(chips)]
        groups = [parts]
        if k == bags - 1 and len(parts) > chips:
            groups = [parts[: chips - 1], parts[chips - 1 :]]
        queries.append([])
        for group in groups:
            query, kv = project(group, weights, head_count)
            queries[k].append(query)
            pieces += [kv, swap(kv, core=1)]
    mixed = [None] * bags
    for k in reversed(range(bags)):
        part, kv = attend(queries[k], pieces, chips, capacity)
        pieces = [kv]
        mixed[k] = swap(part, dz=k) if k else part
    rounds = [[k for k in range(bags) if k != 2], [2]] if bags > 2 else [list(range(bags))]
    shares = []
    for members in rounds:
        for j in range(chips):
            share = jnp.stack([mixed[k][j] for k in members])
            shares.append(swap(share, dx=j // along, dy=j % along) if j else share)
    return finish(tokens, seq_row, modulation, shares, rounds, w_out, w_fc1, w_fc2, capacity, chips)


def solution(mesh):
    placed = (P(("bag", "sp"), None), P(("bag", "sp")), P(), P(), P(), P(), P())
    return jax.shard_map(
        layer, mesh=mesh, in_specs=placed, out_specs=P(("bag", "sp"), None), check_vma=False
    )
```

```python
import functools
import math

import jax
import jax.numpy as jnp
from jax import lax
from jax.experimental import pallas as pl
from jax.experimental.pallas import tpu as pltpu
from jax.sharding import PartitionSpec as P


HD = 72
SEQ_BAG = 1
LANE = 128
EPS = 1e-06
HUGE = 1e30
AXES = ("bag", "sp")
BF16, F32 = jnp.bfloat16, jnp.float32


def vmem():
    return pl.BlockSpec(memory_space=pltpu.VMEM)


def hbm():
    return pl.BlockSpec(memory_space=pltpu.HBM)


def limit(mebibytes):
    return pltpu.CompilerParams(vmem_limit_bytes=mebibytes << 20)


def coordinates():
    along = lax.axis_size("sp") // lax.axis_size("bag")
    bag, sp = lax.axis_index("bag"), lax.axis_index("sp")
    return lax.div(sp, along), lax.div(bag, 2) * along + lax.rem(sp, along)


def layer_norm(values):
    center = values - jnp.mean(values, axis=-1, keepdims=True)
    spread = jnp.mean(center * center, axis=-1, keepdims=True)
    return center * lax.rsqrt(spread + EPS)


def to_column(row):
    n = row.shape[1]
    diagonal = lax.broadcasted_iota(jnp.int32, (n, n), 0) == lax.broadcasted_iota(jnp.int32, (n, n), 1)
    return jnp.sum(jnp.where(diagonal, jnp.broadcast_to(row, (n, n)), 0.0), axis=1, keepdims=True)


def slot_of_row(bag_row, capacity):
    n = bag_row.shape[1]
    earlier = lax.broadcasted_iota(jnp.int32, (n, n), 0) < lax.broadcasted_iota(jnp.int32, (n, n), 1)
    same = jnp.broadcast_to(to_column(bag_row), (n, n)) == jnp.broadcast_to(bag_row, (n, n))
    rank = jnp.sum(jnp.where(same & earlier, 1.0, 0.0), axis=0, keepdims=True)
    return (bag_row * capacity + rank).astype(jnp.int32)


def slot_kernel(capacity, tokens_ref, seq_ref, mod_ref, *out_refs):
    me, _ = coordinates()
    row_count, width = tokens_ref.shape
    block_count = len(out_refs)
    bag_row = ((seq_ref[...] // SEQ_BAG) ^ me).astype(F32)
    position = slot_of_row(bag_row, capacity)
    slot_ids = lax.broadcasted_iota(jnp.int32, (block_count * capacity, row_count), 0)
    pick = jnp.where(slot_ids == position, 1.0, 0.0)
    filled = jnp.sum(pick, axis=1, keepdims=True)
    rows = jnp.dot(pick.astype(BF16), tokens_ref[...], preferred_element_type=F32)
    first = lax.broadcasted_iota(jnp.int32, (capacity, width), 1) == 0
    for block, out_ref in enumerate(out_refs):
        part = slice(block * capacity, (block + 1) * capacity)
        shift, scale = [mod_ref[column, pl.ds(block ^ me, 1)] for column in (0, 1)]
        normed = layer_norm(rows[part]) * (1.0 + scale) + shift
        normed = jnp.where(first & (filled[part] < 0.5), HUGE, normed)
        out_ref[...] = normed.astype(BF16)


def slot_rows(tokens, seq_row, modulation, bag_count, capacity):
    width = tokens.shape[1]
    return pl.pallas_call(
        functools.partial(slot_kernel, capacity),
        in_specs=[vmem(), vmem(), vmem()],
        out_specs=[vmem()] * bag_count,
        out_shape=[jax.ShapeDtypeStruct((capacity, width), BF16)] * bag_count,
        compiler_params=limit(16),
        name="slot_rows",
    )(tokens, seq_row, modulation)


def weight_kernel(part, w_ref, out_ref, window, sem):
    total = w_ref.shape[1]
    wide = window.shape[2]
    copies, shifts = [], []
    _, chip = coordinates()
    for kind in range(3):
        start = kind * (total // 3) + chip * part
        base = pl.multiple_of(jnp.minimum(start // LANE * LANE, total - wide), LANE)
        shifts.append(start - base)
        copies.append(
            pltpu.make_async_copy(w_ref.at[:, pl.ds(base, wide)], window.at[kind], sem.at[kind])
        )
    for copy in copies:
        copy.start()
    pieces = []
    for kind, copy in enumerate(copies):
        copy.wait()
        rolled = pltpu.roll(window[kind].astype(F32), wide - shifts[kind], axis=1)
        pieces.append(rolled[:, :part].astype(BF16))
    filler = out_ref.shape[1] - 3 * part
    if filler:
        pieces.append(jnp.zeros((w_ref.shape[0], filler), BF16))
    out_ref[...] = jnp.concatenate(pieces, axis=1)


def round_up(value, unit):
    return -(-value // unit) * unit


def chip_weights(w_qkv, head_count):
    depth, part = w_qkv.shape[0], head_count * HD
    wide = round_up(part + LANE - math.gcd(part, LANE), LANE)
    return pl.pallas_call(
        functools.partial(weight_kernel, part),
        in_specs=[hbm()],
        out_specs=vmem(),
        out_shape=jax.ShapeDtypeStruct((depth, round_up(3 * part, LANE)), BF16),
        scratch_shapes=[pltpu.VMEM((3, depth, wide), BF16), pltpu.SemaphoreType.DMA((3,))],
        cost_estimate=pl.CostEstimate(flops=10**9, bytes_accessed=10**7, transcendentals=0),
        compiler_params=limit(20),
        name="chip_weights",
    )(w_qkv)


def project_kernel(head_count, *refs):
    w_ref, (q_ref, kv_ref) = refs[-3], refs[-2:]
    rows = jnp.concatenate([ref[...] for ref in refs[:-3]], axis=0)
    size = rows.shape[0]
    factor = math.log2(math.e) / math.sqrt(HD)
    empty = rows[:, :1].astype(F32) > 0.5 * HUGE
    start = jnp.where(empty, 0.0, rows[:, :LANE].astype(F32)).astype(BF16)
    rows = jnp.concatenate([start, rows[:, LANE:]], axis=1)
    made = jnp.dot(rows, w_ref[...], preferred_element_type=F32)
    lane = lax.broadcasted_iota(jnp.int32, (size, LANE), 1)
    bias = jnp.where(empty, -HUGE, 0.0)
    for kind in range(3):
        for head in range(head_count):
            column = (kind * head_count + head) * HD
            base, shift = column // LANE * LANE, column % LANE
            wide = LANE if shift + HD <= LANE else 2 * LANE
            value = made[:, base : base + wide]
            if shift:
                value = pltpu.roll(value, wide - shift, axis=1)
            value = value[:, :LANE]
            if kind == 0:
                value, beside = value * factor, 1.0
            else:
                beside = bias if kind == 1 else 1.0
            value = jnp.where(lane < HD, value, jnp.where(lane == HD, beside, 0.0)).astype(BF16)
            if kind == 0:
                q_ref[head] = value
            else:
                kv_ref[kind - 1, head] = value


def project(parts, weights, head_count):
    size, depth = sum(part.shape[0] for part in parts), weights.shape[0]
    return pl.pallas_call(
        functools.partial(project_kernel, head_count),
        in_specs=[vmem()] * (len(parts) + 1),
        out_specs=[vmem(), vmem()],
        out_shape=[
            jax.ShapeDtypeStruct((head_count, size, LANE), BF16),
            jax.ShapeDtypeStruct((2, head_count, size, LANE), BF16),
        ],
        cost_estimate=pl.CostEstimate(
            flops=2 * size * depth * weights.shape[1], bytes_accessed=4 * size * depth, transcendentals=0
        ),
        compiler_params=limit(12),
        name="project",
    )(*parts, weights)


def packed_rows(capacity, width):
    whole = width // LANE
    rest = width - whole * LANE
    if rest == 0:
        return whole * capacity, 0, 0
    if capacity % 16:
        return (whole + 1) * capacity, rest, capacity
    groups = LANE // rest
    tiles = -(-(capacity // 16) // groups)
    return whole * capacity + tiles * 16, rest, 16


def pack(block, write):
    capacity, width = block.shape
    whole = width // LANE
    for tile in range(whole):
        write(tile * capacity, block[:, tile * LANE : (tile + 1) * LANE])
    _, rest, size = packed_rows(capacity, width)
    if rest == 0:
        return
    tail = block[:, whole * LANE :]
    groups = 1 if size == capacity else LANE // rest
    for first in range(0, capacity // size, groups):
        pieces = [
            tail[group * size : (group + 1) * size]
            for group in range(first, min(first + groups, capacity // size))
        ]
        filler = LANE - rest * len(pieces)
        if filler:
            pieces.append(jnp.zeros((size, filler), block.dtype))
        write(whole * capacity + first // groups * size, jnp.concatenate(pieces, axis=1))


def unpack(packed, capacity, width):
    whole = width // LANE
    columns = [packed[tile * capacity : (tile + 1) * capacity] for tile in range(whole)]
    _, rest, size = packed_rows(capacity, width)
    if rest:
        groups = 1 if size == capacity else LANE // rest
        pieces = []
        for group in range(capacity // size):
            top = whole * capacity + group // groups * size
            left = group % groups * rest
            pieces.append(packed[top : top + size, left : left + rest])
        columns.append(jnp.concatenate(pieces, axis=0))
    return jnp.concatenate(columns, axis=1)


def attend_kernel(chips, capacity, first_row, query_count, piece_count, *refs):
    queries, pieces = refs[:query_count], refs[query_count : query_count + piece_count]
    out_ref = refs[query_count + piece_count]
    if piece_count > 1:
        kv_ref = refs[-1]
        at = 0
        for ref in pieces:
            kv_ref[:, :, at : at + ref.shape[2]] = ref[...]
            at += ref.shape[2]
    else:
        kv_ref = pieces[0]
    nt = (((1,), (1,)), ((), ()))
    results = []
    for head in range(kv_ref.shape[1]):
        query = jnp.concatenate([ref[head] for ref in queries], axis=0)
        query = query[first_row : first_row + chips * capacity]
        score = lax.dot_general(query, kv_ref[0, head], nt, preferred_element_type=F32)
        top = jnp.max(score, axis=1, keepdims=True)
        probs = jnp.exp2(score - top).astype(BF16)
        mixed = jnp.dot(probs, kv_ref[1, head], preferred_element_type=F32)
        results.append(mixed[:, :HD] / mixed[:, HD : HD + 1])
    rows = jnp.concatenate(results, axis=1).astype(BF16)
    for chip in range(chips):
        block = rows[chip * capacity : (chip + 1) * capacity]

        def write(first, value):
            out_ref[chip, first : first + value.shape[0]] = value

        pack(block, write)


def attend(queries, pieces, chips, capacity, index, halves):
    chips //= halves
    head_count, rows = queries[0].shape[0], chips * capacity
    keys = sum(piece.shape[2] for piece in pieces)
    out_rows = packed_rows(capacity, head_count * HD)[0]
    out_shape = [jax.ShapeDtypeStruct((chips, out_rows, LANE), BF16)]
    if len(pieces) > 1:
        out_shape.append(jax.ShapeDtypeStruct((2, head_count, keys, LANE), BF16))
    made = pl.pallas_call(
        functools.partial(attend_kernel, chips, capacity, index * rows, len(queries), len(pieces)),
        in_specs=[vmem()] * (len(queries) + len(pieces)),
        out_specs=[vmem()] * len(out_shape),
        out_shape=out_shape,
        cost_estimate=pl.CostEstimate(
            flops=4 * head_count * rows * keys * LANE,
            bytes_accessed=4 * head_count * keys * LANE,
            transcendentals=head_count * rows * keys,
        ),
        compiler_params=limit(24),
        name="attend",
    )(*queries, *pieces)
    return made[0], (made[1] if len(pieces) > 1 else pieces[0])


def finish_kernel(capacity, chips, rounds, tokens_ref, seq_ref, mod_ref, w_out, w_fc1, w_fc2, *refs):
    parts, out_ref, whole = refs[:-2], refs[-2], refs[-1]
    row_count, width = tokens_ref.shape
    plane, here = coordinates()
    for index, part in enumerate(parts):
        for at, bag in enumerate(rounds[index // chips]):
            whole[here ^ (index % chips), bag] = part[at]
    bags = whole.shape[1]
    seq_row = seq_ref[...]
    position = slot_of_row(((seq_row // SEQ_BAG) ^ plane).astype(F32), capacity)
    slot_ids = lax.broadcasted_iota(jnp.int32, (bags * capacity, row_count), 0)
    pick = jnp.where(slot_ids == position, 1.0, 0.0).astype(BF16)
    seq_column = to_column(seq_row.astype(F32))
    slots = jnp.concatenate(
        [
            jnp.concatenate(
                [unpack(whole[chip, bag], capacity, width // chips) for chip in range(chips)], axis=1
            )
            for bag in range(bags)
        ],
        axis=0,
    )
    tn = (((0,), (0,)), ((), ()))
    attended = lax.dot_general(pick, slots, tn, preferred_element_type=F32).astype(BF16)

    def per_row(column):
        value = jnp.broadcast_to(mod_ref[column, 0:1], (row_count, width))
        for seq in range(1, mod_ref.shape[1]):
            value = jnp.where(seq_column == seq, mod_ref[column, seq : seq + 1], value)
        return value

    branch = jnp.dot(attended, w_out[...], preferred_element_type=F32)
    hidden = (tokens_ref[...].astype(F32) + per_row(2) * branch).astype(BF16)
    normed = (layer_norm(hidden.astype(F32)) * (1.0 + per_row(4)) + per_row(3)).astype(BF16)
    active = jax.nn.gelu(jnp.dot(normed, w_fc1[...], preferred_element_type=F32), approximate=True)
    last = jnp.dot(active.astype(BF16), w_fc2[...], preferred_element_type=F32)
    out_ref[...] = (hidden.astype(F32) + per_row(5) * last).astype(BF16)


def finish(tokens, seq_row, modulation, parts, rounds, w_out, w_fc1, w_fc2, capacity, chips):
    bags = sum(len(members) for members in rounds)
    return pl.pallas_call(
        functools.partial(finish_kernel, capacity, chips, rounds),
        in_specs=[vmem()] * (6 + len(parts)),
        out_specs=vmem(),
        out_shape=jax.ShapeDtypeStruct(tokens.shape, BF16),
        scratch_shapes=[pltpu.VMEM((chips, bags) + parts[0].shape[1:], BF16)],
        compiler_params=limit(20),
        name="finish",
    )(tokens, seq_row, modulation, w_out, w_fc1, w_fc2, *parts)


def layer(tokens, row_seq, modulation, w_qkv, w_out, w_fc1, w_fc2):
    bags, sp = lax.axis_size("bag"), lax.axis_size("sp")
    along, across, cores = sp // bags, bags // 2, 2
    chips = across * along
    row_count, width = tokens.shape
    capacity = row_count // bags * 5 // 4
    head_count = width // HD // chips

    def swap(value, dx=0, core=0, dz=0, dy=0):
        pairs = []
        for b in range(bags):
            for s in range(sp):
                b2 = ((b // cores) ^ dx) * cores + ((b % cores) ^ core)
                s2 = ((s // along) ^ dz) * along + ((s % along) ^ dy)
                pairs.append((b * sp + s, b2 * sp + s2))
        return lax.ppermute(value, AXES, pairs)

    seq_row = row_seq.reshape(1, row_count)
    modulation = jnp.transpose(modulation, (1, 0, 2))

    def in_place(value):
        return pltpu.with_memory_space_constraint(value, pltpu.HBM)

    blocks = slot_rows(in_place(tokens), in_place(seq_row), in_place(modulation), bags, capacity)
    weights = chip_weights(in_place(w_qkv), head_count)
    blocks = [block if k == 0 else swap(block, dz=k) for k, block in enumerate(blocks)]
    half = round_up(capacity, 32) // 2
    queries, pieces = [], []
    for k, block in enumerate(blocks):
        if across == 2 and along == 2:
            from_x, from_y = swap(block, dx=1), swap(block, dy=1)
            upper, lower = swap(from_x[:half], dy=1), swap(from_y[half:], dx=1)
            parts = [block, from_y, from_x, upper, lower]
        else:
            parts = [swap(block, dx=j // along, dy=j % along) if j else block for j in range(chips)]
        groups = [parts]
        if k == bags - 1 and len(parts) > chips:
            groups = [parts[: chips - 1], parts[chips - 1 :]]
        queries.append([])
        for group in groups:
            query, kv = project(group, weights, head_count)
            queries[k].append(query)
            pieces += [kv, swap(kv, core=1)]
    mixed = [None] * bags
    rounds = [[bags - 1], [k for k in range(bags - 1) if k != 2], [2]] if bags > 3 else [list(range(bags))]
    shares = []

    def exchange(index):
        for j in range(chips):
            share = jnp.stack([mixed[k][j] for k in rounds[index]])
            shares.append(swap(share, dx=j // along, dy=j % along) if j else share)

    for k in reversed(range(bags)):
        halves = 2 if k == bags - 1 and chips % 2 == 0 else 1
        mixed[k] = []
        for index in range(halves):
            part, kv = attend(queries[k], pieces, chips, capacity, index, halves)
            pieces = [kv]
            part = swap(part, dz=k) if k else part
            mixed[k] += [part[j] for j in range(part.shape[0])]
    for index in range(len(rounds)):
        exchange(index)
    return finish(
        tokens, seq_row, modulation, shares, rounds, w_out, w_fc1, w_fc2, capacity, chips
    )


def solution(mesh):
    placed = (P(("bag", "sp"), None), P(("bag", "sp")), P(), P(), P(), P(), P())
    return jax.shard_map(layer, mesh=mesh, in_specs=placed, out_specs=P(("bag", "sp"), None), check_vma=False)
```

```python
import functools
import math

import jax
import jax.numpy as jnp
from jax import lax
from jax.experimental import pallas as pl
from jax.experimental.pallas import tpu as pltpu
from jax.sharding import PartitionSpec as P


HD = 72
SEQ_BAG = 1
LANE = 128
EPS = 1e-06
HUGE = 1e30
AXES = ("bag", "sp")
BF16, F32 = jnp.bfloat16, jnp.float32


def vmem():
    return pl.BlockSpec(memory_space=pltpu.VMEM)


def hbm():
    return pl.BlockSpec(memory_space=pltpu.HBM)


def limit(mebibytes):
    return pltpu.CompilerParams(vmem_limit_bytes=mebibytes << 20)


def coordinates():
    along = lax.axis_size("sp") // lax.axis_size("bag")
    bag, sp = lax.axis_index("bag"), lax.axis_index("sp")
    return lax.div(sp, along), lax.div(bag, 2) * along + lax.rem(sp, along)


def layer_norm(values):
    center = values - jnp.mean(values, axis=-1, keepdims=True)
    spread = jnp.mean(center * center, axis=-1, keepdims=True)
    return center * lax.rsqrt(spread + EPS)


def to_column(row):
    n = row.shape[1]
    diagonal = lax.broadcasted_iota(jnp.int32, (n, n), 0) == lax.broadcasted_iota(jnp.int32, (n, n), 1)
    return jnp.sum(jnp.where(diagonal, jnp.broadcast_to(row, (n, n)), 0.0), axis=1, keepdims=True)


def slot_of_row(bag_row, capacity):
    n = bag_row.shape[1]
    earlier = lax.broadcasted_iota(jnp.int32, (n, n), 0) < lax.broadcasted_iota(jnp.int32, (n, n), 1)
    same = jnp.broadcast_to(to_column(bag_row), (n, n)) == jnp.broadcast_to(bag_row, (n, n))
    rank = jnp.sum(jnp.where(same & earlier, 1.0, 0.0), axis=0, keepdims=True)
    return (bag_row * capacity + rank).astype(jnp.int32)


def round_up(value, unit):
    return -(-value // unit) * unit


def window_base(start, total, wide):
    aligned, last = start // LANE * LANE, total - wide
    return min(aligned, last) if isinstance(start, int) else jnp.minimum(aligned, last)


def slot_kernel(capacity, part, tokens_ref, seq_ref, mod_ref, w_ref, window_ref, *refs):
    out_refs, sem = refs[:-1], refs[-1]
    me, chip = coordinates()
    total, wide = w_ref.shape[1], window_ref.shape[2]
    copies = []
    for kind in range(3):
        base = pl.multiple_of(window_base(kind * (total // 3) + chip * part, total, wide), LANE)
        copies.append(
            pltpu.make_async_copy(w_ref.at[:, pl.ds(base, wide)], window_ref.at[kind], sem.at[kind])
        )
    for copy in copies:
        copy.start()
    row_count, width = tokens_ref.shape
    block_count = len(out_refs)
    bag_row = ((seq_ref[...] // SEQ_BAG) ^ me).astype(F32)
    position = slot_of_row(bag_row, capacity)
    slot_ids = lax.broadcasted_iota(jnp.int32, (block_count * capacity, row_count), 0)
    pick = jnp.where(slot_ids == position, 1.0, 0.0)
    filled = jnp.sum(pick, axis=1, keepdims=True)
    rows = jnp.dot(pick.astype(BF16), tokens_ref[...], preferred_element_type=F32)
    first = lax.broadcasted_iota(jnp.int32, (capacity, width), 1) == 0
    for block, out_ref in enumerate(out_refs):
        rows_of = slice(block * capacity, (block + 1) * capacity)
        shift, scale = [mod_ref[column, pl.ds(block ^ me, 1)] for column in (0, 1)]
        normed = layer_norm(rows[rows_of]) * (1.0 + scale) + shift
        normed = jnp.where(first & (filled[rows_of] < 0.5), HUGE, normed)
        out_ref[...] = normed.astype(BF16)
    for copy in copies:
        copy.wait()


def slot_rows(tokens, seq_row, modulation, w_qkv, bag_count, capacity, part):
    width = tokens.shape[1]
    wide = round_up(part + LANE - math.gcd(part, LANE), LANE)
    made = pl.pallas_call(
        functools.partial(slot_kernel, capacity, part),
        in_specs=[vmem(), vmem(), vmem(), hbm()],
        out_specs=[vmem()] * (1 + bag_count),
        out_shape=[jax.ShapeDtypeStruct((3, w_qkv.shape[0], wide), BF16)]
        + [jax.ShapeDtypeStruct((capacity, width), BF16)] * bag_count,
        scratch_shapes=[pltpu.SemaphoreType.DMA((3,))],
        compiler_params=limit(16),
        name="slot_rows",
    )(tokens, seq_row, modulation, w_qkv)
    return made[0], made[1:]


def weight_kernel(part, total, chips, window_ref, out_ref):
    _, here = coordinates()
    depth, wide = window_ref.shape[1:]
    for chip in range(chips):

        @pl.when(here == chip)
        def _():
            pieces = []
            for kind in range(3):
                start = kind * (total // 3) + chip * part
                shift = start - window_base(start, total, wide)
                pieces.append(window_ref[kind][:, shift : shift + part])
            filler = out_ref.shape[1] - 3 * part
            if filler:
                pieces.append(jnp.zeros((depth, filler), BF16))
            out_ref[...] = jnp.concatenate(pieces, axis=1)


def chip_weights(windows, total, part):
    depth = windows.shape[1]
    return pl.pallas_call(
        functools.partial(weight_kernel, part, total, total // 3 // part),
        in_specs=[vmem()],
        out_specs=vmem(),
        out_shape=jax.ShapeDtypeStruct((depth, round_up(3 * part, LANE)), BF16),
        cost_estimate=pl.CostEstimate(flops=10**9, bytes_accessed=10**7, transcendentals=0),
        compiler_params=limit(16),
        name="chip_weights",
    )(windows)


def project_kernel(head_count, *refs):
    w_ref, (q_ref, kv_ref) = refs[-3], refs[-2:]
    rows = jnp.concatenate([ref[...] for ref in refs[:-3]], axis=0)
    size = rows.shape[0]
    factor = math.log2(math.e) / math.sqrt(HD)
    empty = rows[:, :1].astype(F32) > 0.5 * HUGE
    start = jnp.where(empty, 0.0, rows[:, :LANE].astype(F32)).astype(BF16)
    rows = jnp.concatenate([start, rows[:, LANE:]], axis=1)
    made = jnp.dot(rows, w_ref[...], preferred_element_type=F32)
    lane = lax.broadcasted_iota(jnp.int32, (size, LANE), 1)
    bias = jnp.where(empty, -HUGE, 0.0)
    for kind in range(3):
        for head in range(head_count):
            column = (kind * head_count + head) * HD
            base, shift = column // LANE * LANE, column % LANE
            wide = LANE if shift + HD <= LANE else 2 * LANE
            value = made[:, base : base + wide]
            if shift:
                value = pltpu.roll(value, wide - shift, axis=1)
            value = value[:, :LANE]
            if kind == 0:
                value, beside = value * factor, 1.0
            else:
                beside = bias if kind == 1 else 1.0
            value = jnp.where(lane < HD, value, jnp.where(lane == HD, beside, 0.0)).astype(BF16)
            if kind == 0:
                q_ref[head] = value
            else:
                kv_ref[kind - 1, head] = value


def project(parts, weights, head_count):
    size, depth = sum(part.shape[0] for part in parts), weights.shape[0]
    return pl.pallas_call(
        functools.partial(project_kernel, head_count),
        in_specs=[vmem()] * (len(parts) + 1),
        out_specs=[vmem(), vmem()],
        out_shape=[
            jax.ShapeDtypeStruct((head_count, size, LANE), BF16),
            jax.ShapeDtypeStruct((2, head_count, size, LANE), BF16),
        ],
        cost_estimate=pl.CostEstimate(
            flops=2 * size * depth * weights.shape[1], bytes_accessed=4 * size * depth, transcendentals=0
        ),
        compiler_params=limit(12),
        name="project",
    )(*parts, weights)


def packed_rows(capacity, width):
    whole = width // LANE
    rest = width - whole * LANE
    if rest == 0:
        return whole * capacity, 0, 0
    if capacity % 16:
        return (whole + 1) * capacity, rest, capacity
    groups = LANE // rest
    tiles = -(-(capacity // 16) // groups)
    return whole * capacity + tiles * 16, rest, 16


def pack(block, write):
    capacity, width = block.shape
    whole = width // LANE
    for tile in range(whole):
        write(tile * capacity, block[:, tile * LANE : (tile + 1) * LANE])
    _, rest, size = packed_rows(capacity, width)
    if rest == 0:
        return
    tail = block[:, whole * LANE :]
    groups = 1 if size == capacity else LANE // rest
    for first in range(0, capacity // size, groups):
        pieces = [
            tail[group * size : (group + 1) * size]
            for group in range(first, min(first + groups, capacity // size))
        ]
        filler = LANE - rest * len(pieces)
        if filler:
            pieces.append(jnp.zeros((size, filler), block.dtype))
        write(whole * capacity + first // groups * size, jnp.concatenate(pieces, axis=1))


def unpack(packed, capacity, width):
    whole = width // LANE
    columns = [packed[tile * capacity : (tile + 1) * capacity] for tile in range(whole)]
    _, rest, size = packed_rows(capacity, width)
    if rest:
        groups = 1 if size == capacity else LANE // rest
        pieces = []
        for group in range(capacity // size):
            top = whole * capacity + group // groups * size
            left = group % groups * rest
            pieces.append(packed[top : top + size, left : left + rest])
        columns.append(jnp.concatenate(pieces, axis=0))
    return jnp.concatenate(columns, axis=1)


def attend_kernel(chips, capacity, first_row, query_count, piece_count, *refs):
    queries, pieces = refs[:query_count], refs[query_count : query_count + piece_count]
    out_ref = refs[query_count + piece_count]
    if piece_count > 1:
        kv_ref = refs[-1]
        at = 0
        for ref in pieces:
            kv_ref[:, :, at : at + ref.shape[2]] = ref[...]
            at += ref.shape[2]
    else:
        kv_ref = pieces[0]
    nt = (((1,), (1,)), ((), ()))
    results = []
    for head in range(kv_ref.shape[1]):
        query = jnp.concatenate([ref[head] for ref in queries], axis=0)
        query = query[first_row : first_row + chips * capacity]
        score = lax.dot_general(query, kv_ref[0, head], nt, preferred_element_type=F32)
        top = jnp.max(score, axis=1, keepdims=True)
        probs = jnp.exp2(score - top).astype(BF16)
        mixed = jnp.dot(probs, kv_ref[1, head], preferred_element_type=F32)
        results.append(mixed[:, :HD] / mixed[:, HD : HD + 1])
    rows = jnp.concatenate(results, axis=1).astype(BF16)
    for chip in range(chips):
        block = rows[chip * capacity : (chip + 1) * capacity]

        def write(first, value):
            out_ref[chip, first : first + value.shape[0]] = value

        pack(block, write)


def attend(queries, pieces, chips, capacity, index, halves):
    chips //= halves
    head_count, rows = queries[0].shape[0], chips * capacity
    keys = sum(piece.shape[2] for piece in pieces)
    out_rows = packed_rows(capacity, head_count * HD)[0]
    out_shape = [jax.ShapeDtypeStruct((chips, out_rows, LANE), BF16)]
    if len(pieces) > 1:
        out_shape.append(jax.ShapeDtypeStruct((2, head_count, keys, LANE), BF16))
    made = pl.pallas_call(
        functools.partial(attend_kernel, chips, capacity, index * rows, len(queries), len(pieces)),
        in_specs=[vmem()] * (len(queries) + len(pieces)),
        out_specs=[vmem()] * len(out_shape),
        out_shape=out_shape,
        cost_estimate=pl.CostEstimate(
            flops=4 * head_count * rows * keys * LANE,
            bytes_accessed=4 * head_count * keys * LANE,
            transcendentals=head_count * rows * keys,
        ),
        compiler_params=limit(24),
        name="attend",
    )(*queries, *pieces)
    return made[0], (made[1] if len(pieces) > 1 else pieces[0])


def finish_kernel(capacity, chips, rounds, tokens_ref, seq_ref, mod_ref, w_out, w_fc1, w_fc2, *refs):
    parts, out_ref, whole = refs[:-2], refs[-2], refs[-1]
    row_count, width = tokens_ref.shape
    plane, here = coordinates()
    for index, part in enumerate(parts):
        for at, bag in enumerate(rounds[index // chips]):
            whole[here ^ (index % chips), bag] = part[at]
    bags = whole.shape[1]
    seq_row = seq_ref[...]
    position = slot_of_row(((seq_row // SEQ_BAG) ^ plane).astype(F32), capacity)
    slot_ids = lax.broadcasted_iota(jnp.int32, (bags * capacity, row_count), 0)
    pick = jnp.where(slot_ids == position, 1.0, 0.0).astype(BF16)
    seq_column = to_column(seq_row.astype(F32))
    slots = jnp.concatenate(
        [
            jnp.concatenate(
                [unpack(whole[chip, bag], capacity, width // chips) for chip in range(chips)], axis=1
            )
            for bag in range(bags)
        ],
        axis=0,
    )
    tn = (((0,), (0,)), ((), ()))
    attended = lax.dot_general(pick, slots, tn, preferred_element_type=F32).astype(BF16)

    def per_row(column):
        value = jnp.broadcast_to(mod_ref[column, 0:1], (row_count, width))
        for seq in range(1, mod_ref.shape[1]):
            value = jnp.where(seq_column == seq, mod_ref[column, seq : seq + 1], value)
        return value

    branch = jnp.dot(attended, w_out[...], preferred_element_type=F32)
    hidden = (tokens_ref[...].astype(F32) + per_row(2) * branch).astype(BF16)
    normed = (layer_norm(hidden.astype(F32)) * (1.0 + per_row(4)) + per_row(3)).astype(BF16)
    active = jax.nn.gelu(jnp.dot(normed, w_fc1[...], preferred_element_type=F32), approximate=True)
    last = jnp.dot(active.astype(BF16), w_fc2[...], preferred_element_type=F32)
    out_ref[...] = (hidden.astype(F32) + per_row(5) * last).astype(BF16)


def finish(tokens, seq_row, modulation, parts, rounds, w_out, w_fc1, w_fc2, capacity, chips):
    bags = sum(len(members) for members in rounds)
    return pl.pallas_call(
        functools.partial(finish_kernel, capacity, chips, rounds),
        in_specs=[vmem()] * (6 + len(parts)),
        out_specs=vmem(),
        out_shape=jax.ShapeDtypeStruct(tokens.shape, BF16),
        scratch_shapes=[pltpu.VMEM((chips, bags) + parts[0].shape[1:], BF16)],
        compiler_params=limit(20),
        name="finish",
    )(tokens, seq_row, modulation, w_out, w_fc1, w_fc2, *parts)


def layer(tokens, row_seq, modulation, w_qkv, w_out, w_fc1, w_fc2):
    bags, sp = lax.axis_size("bag"), lax.axis_size("sp")
    along, across, cores = sp // bags, bags // 2, 2
    chips = across * along
    row_count, width = tokens.shape
    capacity = row_count // bags * 5 // 4
    head_count = width // HD // chips

    def swap(value, dx=0, core=0, dz=0, dy=0):
        pairs = []
        for b in range(bags):
            for s in range(sp):
                b2 = ((b // cores) ^ dx) * cores + ((b % cores) ^ core)
                s2 = ((s // along) ^ dz) * along + ((s % along) ^ dy)
                pairs.append((b * sp + s, b2 * sp + s2))
        return lax.ppermute(value, AXES, pairs)

    seq_row = row_seq.reshape(1, row_count)
    modulation = jnp.transpose(modulation, (1, 0, 2))

    def in_place(value):
        return pltpu.with_memory_space_constraint(value, pltpu.HBM)

    inputs = [in_place(value) for value in (tokens, seq_row, modulation, w_qkv)]
    windows, blocks = slot_rows(*inputs, bags, capacity, head_count * HD)
    weights = chip_weights(windows, w_qkv.shape[1], head_count * HD)
    blocks = [block if k == 0 else swap(block, dz=k) for k, block in enumerate(blocks)]
    half = round_up(capacity, 32) // 2
    queries, pieces = [], []
    for k, block in enumerate(blocks):
        if across == 2 and along == 2:
            from_x, from_y = swap(block, dx=1), swap(block, dy=1)
            upper, lower = swap(from_x[:half], dy=1), swap(from_y[half:], dx=1)
            parts = [block, from_y, from_x, upper, lower]
        else:
            parts = [swap(block, dx=j // along, dy=j % along) if j else block for j in range(chips)]
        groups = [parts]
        if k == bags - 1 and len(parts) > chips:
            groups = [parts[: chips - 1], parts[chips - 1 :]]
        queries.append([])
        for group in groups:
            query, kv = project(group, weights, head_count)
            queries[k].append(query)
            pieces += [kv, swap(kv, core=1)]
    mixed = [None] * bags
    rounds = [[bags - 1, 0], list(range(1, bags - 1))] if bags > 2 else [list(range(bags))]
    shares = []

    def exchange(index):
        for j in range(chips):
            share = jnp.stack([mixed[k][j] for k in rounds[index]])
            shares.append(swap(share, dx=j // along, dy=j % along) if j else share)

    for k in reversed(range(bags)):
        halves = 1
        mixed[k] = []
        for index in range(halves):
            part, kv = attend(queries[k], pieces, chips, capacity, index, halves)
            pieces = [kv]
            part = swap(part, dz=k) if k else part
            mixed[k] += [part[j] for j in range(part.shape[0])]
    for index in range(len(rounds)):
        exchange(index)
    return finish(tokens, seq_row, modulation, shares, rounds, w_out, w_fc1, w_fc2, capacity, chips)


def solution(mesh):
    placed = (P(("bag", "sp"), None), P(("bag", "sp")), P(), P(), P(), P(), P())
    return jax.shard_map(
        layer, mesh=mesh, in_specs=placed, out_specs=P(("bag", "sp"), None), check_vma=False
    )
```

```python
import functools
import math

import jax
import jax.numpy as jnp
from jax import lax
from jax.experimental import pallas as pl
from jax.experimental.pallas import tpu as pltpu
from jax.sharding import PartitionSpec as P


HD = 72
SEQ_BAG = 1
LANE = 128
EPS = 1e-06
HUGE = 1e30
AXES = ("bag", "sp")
BF16, F32 = jnp.bfloat16, jnp.float32


def vmem():
    return pl.BlockSpec(memory_space=pltpu.VMEM)


def hbm():
    return pl.BlockSpec(memory_space=pltpu.HBM)


def limit(mebibytes):
    return pltpu.CompilerParams(vmem_limit_bytes=mebibytes << 20)


def coordinates():
    along = lax.axis_size("sp") // lax.axis_size("bag")
    bag, sp = lax.axis_index("bag"), lax.axis_index("sp")
    return lax.div(sp, along), lax.div(bag, 2) * along + lax.rem(sp, along)


def layer_norm(values):
    center = values - jnp.mean(values, axis=-1, keepdims=True)
    spread = jnp.mean(center * center, axis=-1, keepdims=True)
    return center * lax.rsqrt(spread + EPS)


def to_column(row):
    n = row.shape[1]
    diagonal = lax.broadcasted_iota(jnp.int32, (n, n), 0) == lax.broadcasted_iota(jnp.int32, (n, n), 1)
    return jnp.sum(jnp.where(diagonal, jnp.broadcast_to(row, (n, n)), 0.0), axis=1, keepdims=True)


def slot_of_row(bag_row, capacity):
    n = bag_row.shape[1]
    earlier = lax.broadcasted_iota(jnp.int32, (n, n), 0) < lax.broadcasted_iota(jnp.int32, (n, n), 1)
    same = jnp.broadcast_to(to_column(bag_row), (n, n)) == jnp.broadcast_to(bag_row, (n, n))
    rank = jnp.sum(jnp.where(same & earlier, 1.0, 0.0), axis=0, keepdims=True)
    return (bag_row * capacity + rank).astype(jnp.int32)


def round_up(value, unit):
    return -(-value // unit) * unit


def window_base(start, total, wide):
    aligned, last = start // LANE * LANE, total - wide
    return min(aligned, last) if isinstance(start, int) else jnp.minimum(aligned, last)


def slot_kernel(capacity, tokens_ref, seq_ref, mod_ref, *out_refs):
    me, _ = coordinates()
    row_count, width = tokens_ref.shape
    block_count = len(out_refs)
    bag_row = ((seq_ref[...] // SEQ_BAG) ^ me).astype(F32)
    position = slot_of_row(bag_row, capacity)
    slot_ids = lax.broadcasted_iota(jnp.int32, (block_count * capacity, row_count), 0)
    pick = jnp.where(slot_ids == position, 1.0, 0.0)
    filled = jnp.sum(pick, axis=1, keepdims=True)
    rows = jnp.dot(pick.astype(BF16), tokens_ref[...], preferred_element_type=F32)
    first = lax.broadcasted_iota(jnp.int32, (capacity, width), 1) == 0
    for block, out_ref in enumerate(out_refs):
        rows_of = slice(block * capacity, (block + 1) * capacity)
        shift, scale = [mod_ref[column, pl.ds(block ^ me, 1)] for column in (0, 1)]
        normed = layer_norm(rows[rows_of]) * (1.0 + scale) + shift
        normed = jnp.where(first & (filled[rows_of] < 0.5), HUGE, normed)
        out_ref[...] = normed.astype(BF16)


def slot_rows(tokens, seq_row, modulation, bag_count, capacity):
    width = tokens.shape[1]
    return pl.pallas_call(
        functools.partial(slot_kernel, capacity),
        in_specs=[vmem(), vmem(), vmem()],
        out_specs=[vmem()] * bag_count,
        out_shape=[jax.ShapeDtypeStruct((capacity, width), BF16)] * bag_count,
        compiler_params=limit(16),
        name="slot_rows",
    )(tokens, seq_row, modulation)


def weight_kernel(part, chips, w_ref, out_ref, window_ref, sem):
    _, here = coordinates()
    depth, wide = window_ref.shape[1:]
    total = w_ref.shape[1]
    copies = []
    for kind in range(3):
        base = pl.multiple_of(window_base(kind * (total // 3) + here * part, total, wide), LANE)
        copies.append(
            pltpu.make_async_copy(w_ref.at[:, pl.ds(base, wide)], window_ref.at[kind], sem.at[kind])
        )
    for copy in copies:
        copy.start()
    for copy in copies:
        copy.wait()
    for chip in range(chips):

        @pl.when(here == chip)
        def _():
            pieces = []
            for kind in range(3):
                start = kind * (total // 3) + chip * part
                shift = start - window_base(start, total, wide)
                pieces.append(window_ref[kind][:, shift : shift + part])
            filler = out_ref.shape[1] - 3 * part
            if filler:
                pieces.append(jnp.zeros((depth, filler), BF16))
            out_ref[...] = jnp.concatenate(pieces, axis=1)


def chip_weights(w_qkv, part):
    depth, total = w_qkv.shape
    wide = round_up(part + LANE - math.gcd(part, LANE), LANE)
    return pl.pallas_call(
        functools.partial(weight_kernel, part, total // 3 // part),
        in_specs=[hbm()],
        out_specs=vmem(),
        out_shape=jax.ShapeDtypeStruct((depth, round_up(3 * part, LANE)), BF16),
        scratch_shapes=[pltpu.VMEM((3, depth, wide), BF16), pltpu.SemaphoreType.DMA((3,))],
        cost_estimate=pl.CostEstimate(flops=10**9, bytes_accessed=10**7, transcendentals=0),
        compiler_params=limit(16),
        name="chip_weights",
    )(w_qkv)


def project_kernel(head_count, *refs):
    w_ref, (q_ref, kv_ref) = refs[-3], refs[-2:]
    rows = jnp.concatenate([ref[...] for ref in refs[:-3]], axis=0)
    size = rows.shape[0]
    factor = math.log2(math.e) / math.sqrt(HD)
    empty = rows[:, :1].astype(F32) > 0.5 * HUGE
    start = jnp.where(empty, 0.0, rows[:, :LANE].astype(F32)).astype(BF16)
    rows = jnp.concatenate([start, rows[:, LANE:]], axis=1)
    made = jnp.dot(rows, w_ref[...], preferred_element_type=F32)
    lane = lax.broadcasted_iota(jnp.int32, (size, LANE), 1)
    bias = jnp.where(empty, -HUGE, 0.0)
    for kind in range(3):
        for head in range(head_count):
            column = (kind * head_count + head) * HD
            base, shift = column // LANE * LANE, column % LANE
            wide = LANE if shift + HD <= LANE else 2 * LANE
            value = made[:, base : base + wide]
            if shift:
                value = pltpu.roll(value, wide - shift, axis=1)
            value = value[:, :LANE]
            if kind == 0:
                value, beside = value * factor, 1.0
            else:
                beside = bias if kind == 1 else 1.0
            value = jnp.where(lane < HD, value, jnp.where(lane == HD, beside, 0.0)).astype(BF16)
            if kind == 0:
                q_ref[head] = value
            else:
                kv_ref[kind - 1, head] = value


def project(parts, weights, head_count):
    size, depth = sum(part.shape[0] for part in parts), weights.shape[0]
    return pl.pallas_call(
        functools.partial(project_kernel, head_count),
        in_specs=[vmem()] * (len(parts) + 1),
        out_specs=[vmem(), vmem()],
        out_shape=[
            jax.ShapeDtypeStruct((head_count, size, LANE), BF16),
            jax.ShapeDtypeStruct((2, head_count, size, LANE), BF16),
        ],
        cost_estimate=pl.CostEstimate(
            flops=2 * size * depth * weights.shape[1], bytes_accessed=4 * size * depth, transcendentals=0
        ),
        compiler_params=limit(12),
        name="project",
    )(*parts, weights)


def packed_rows(capacity, width):
    whole = width // LANE
    rest = width - whole * LANE
    if rest == 0:
        return whole * capacity, 0, 0
    if capacity % 16:
        return (whole + 1) * capacity, rest, capacity
    groups = LANE // rest
    tiles = -(-(capacity // 16) // groups)
    return whole * capacity + tiles * 16, rest, 16


def pack(block, write):
    capacity, width = block.shape
    whole = width // LANE
    for tile in range(whole):
        write(tile * capacity, block[:, tile * LANE : (tile + 1) * LANE])
    _, rest, size = packed_rows(capacity, width)
    if rest == 0:
        return
    tail = block[:, whole * LANE :]
    groups = 1 if size == capacity else LANE // rest
    for first in range(0, capacity // size, groups):
        pieces = [
            tail[group * size : (group + 1) * size]
            for group in range(first, min(first + groups, capacity // size))
        ]
        filler = LANE - rest * len(pieces)
        if filler:
            pieces.append(jnp.zeros((size, filler), block.dtype))
        write(whole * capacity + first // groups * size, jnp.concatenate(pieces, axis=1))


def unpack(packed, capacity, width):
    whole = width // LANE
    columns = [packed[tile * capacity : (tile + 1) * capacity] for tile in range(whole)]
    _, rest, size = packed_rows(capacity, width)
    if rest:
        groups = 1 if size == capacity else LANE // rest
        pieces = []
        for group in range(capacity // size):
            top = whole * capacity + group // groups * size
            left = group % groups * rest
            pieces.append(packed[top : top + size, left : left + rest])
        columns.append(jnp.concatenate(pieces, axis=0))
    return jnp.concatenate(columns, axis=1)


def attend_kernel(chips, capacity, first_row, query_count, piece_count, *refs):
    queries, pieces = refs[:query_count], refs[query_count : query_count + piece_count]
    out_ref = refs[query_count + piece_count]
    if piece_count > 1:
        kv_ref = refs[-1]
        at = 0
        for ref in pieces:
            kv_ref[:, :, at : at + ref.shape[2]] = ref[...]
            at += ref.shape[2]
    else:
        kv_ref = pieces[0]
    nt = (((1,), (1,)), ((), ()))
    results = []
    for head in range(kv_ref.shape[1]):
        query = jnp.concatenate([ref[head] for ref in queries], axis=0)
        query = query[first_row : first_row + chips * capacity]
        score = lax.dot_general(query, kv_ref[0, head], nt, preferred_element_type=F32)
        top = jnp.max(score, axis=1, keepdims=True)
        probs = jnp.exp2(score - top).astype(BF16)
        mixed = jnp.dot(probs, kv_ref[1, head], preferred_element_type=F32)
        results.append(mixed[:, :HD] / mixed[:, HD : HD + 1])
    rows = jnp.concatenate(results, axis=1).astype(BF16)
    for chip in range(chips):
        block = rows[chip * capacity : (chip + 1) * capacity]

        def write(first, value):
            out_ref[chip, first : first + value.shape[0]] = value

        pack(block, write)


def attend(queries, pieces, chips, capacity, index, halves):
    chips //= halves
    head_count, rows = queries[0].shape[0], chips * capacity
    keys = sum(piece.shape[2] for piece in pieces)
    out_rows = packed_rows(capacity, head_count * HD)[0]
    out_shape = [jax.ShapeDtypeStruct((chips, out_rows, LANE), BF16)]
    if len(pieces) > 1:
        out_shape.append(jax.ShapeDtypeStruct((2, head_count, keys, LANE), BF16))
    made = pl.pallas_call(
        functools.partial(attend_kernel, chips, capacity, index * rows, len(queries), len(pieces)),
        in_specs=[vmem()] * (len(queries) + len(pieces)),
        out_specs=[vmem()] * len(out_shape),
        out_shape=out_shape,
        cost_estimate=pl.CostEstimate(
            flops=4 * head_count * rows * keys * LANE,
            bytes_accessed=4 * head_count * keys * LANE,
            transcendentals=head_count * rows * keys,
        ),
        compiler_params=limit(24),
        name="attend",
    )(*queries, *pieces)
    return made[0], (made[1] if len(pieces) > 1 else pieces[0])


def finish_kernel(capacity, chips, rounds, index, tokens_ref, seq_ref, mod_ref, w_out, w_fc1, w_fc2, *refs):
    parts, earlier, out_ref, whole = refs[:chips], refs[chips:-2], refs[-2], refs[-1]
    members = rounds[index]
    row_count, width = tokens_ref.shape
    plane, here = coordinates()
    for chip, part in enumerate(parts):
        whole[here ^ chip] = part[...]
    position = slot_of_row(((seq_ref[...] // SEQ_BAG) ^ plane).astype(F32), capacity)

    def picks(bags):
        slot_ids = lax.broadcasted_iota(jnp.int32, (capacity, row_count), 0)
        blocks = [jnp.where(slot_ids + bag * capacity == position, 1.0, 0.0) for bag in bags]
        return jnp.concatenate(blocks, axis=0).astype(BF16)

    def per_slot(column):
        rows = [mod_ref[column, pl.ds(bag ^ plane, 1)] for bag in members]
        return jnp.concatenate([jnp.broadcast_to(row, (capacity, width)) for row in rows], axis=0)

    attended = jnp.concatenate(
        [
            jnp.concatenate(
                [unpack(whole[chip, at], capacity, width // chips) for chip in range(chips)], axis=1
            )
            for at in range(len(members))
        ],
        axis=0,
    )
    residual = jnp.dot(picks(members), tokens_ref[...], preferred_element_type=F32)
    branch = jnp.dot(attended, w_out[...], preferred_element_type=F32)
    hidden = (residual + per_slot(2) * branch).astype(BF16)
    normed = (layer_norm(hidden.astype(F32)) * (1.0 + per_slot(4)) + per_slot(3)).astype(BF16)
    active = jax.nn.gelu(jnp.dot(normed, w_fc1[...], preferred_element_type=F32), approximate=True)
    last = jnp.dot(active.astype(BF16), w_fc2[...], preferred_element_type=F32)
    slots = (hidden.astype(F32) + per_slot(5) * last).astype(BF16)
    if index < len(rounds) - 1:
        out_ref[...] = slots
        return
    slots = jnp.concatenate([ref[...] for ref in earlier] + [slots], axis=0)
    tn = (((0,), (0,)), ((), ()))
    pick = picks([bag for bags in rounds for bag in bags])
    out_ref[...] = lax.dot_general(pick, slots, tn, preferred_element_type=F32).astype(BF16)


def finish(tokens, seq_row, modulation, parts, earlier, rounds, index, w_out, w_fc1, w_fc2, capacity):
    chips, slot_count = len(parts), capacity * len(rounds[index])
    final = index == len(rounds) - 1
    width, depth = tokens.shape[1], w_fc1.shape[1]
    return pl.pallas_call(
        functools.partial(finish_kernel, capacity, chips, rounds, index),
        in_specs=[vmem()] * (6 + chips + len(earlier)),
        out_specs=vmem(),
        out_shape=jax.ShapeDtypeStruct(tokens.shape if final else (slot_count, width), BF16),
        scratch_shapes=[pltpu.VMEM((chips,) + parts[0].shape, BF16)],
        cost_estimate=pl.CostEstimate(
            flops=2 * slot_count * width * (width + 2 * depth),
            bytes_accessed=2 * width * (width + 2 * depth),
            transcendentals=slot_count * depth,
        ),
        compiler_params=limit(20),
        name="finish",
    )(tokens, seq_row, modulation, w_out, w_fc1, w_fc2, *parts, *earlier)


def layer(tokens, row_seq, modulation, w_qkv, w_out, w_fc1, w_fc2):
    bags, sp = lax.axis_size("bag"), lax.axis_size("sp")
    along, across, cores = sp // bags, bags // 2, 2
    chips = across * along
    row_count, width = tokens.shape
    capacity = row_count // bags * 5 // 4
    head_count = width // HD // chips

    def swap(value, dx=0, core=0, dz=0, dy=0):
        pairs = []
        for b in range(bags):
            for s in range(sp):
                b2 = ((b // cores) ^ dx) * cores + ((b % cores) ^ core)
                s2 = ((s // along) ^ dz) * along + ((s % along) ^ dy)
                pairs.append((b * sp + s, b2 * sp + s2))
        return lax.ppermute(value, AXES, pairs)

    seq_row = row_seq.reshape(1, row_count)
    modulation = jnp.transpose(modulation, (1, 0, 2))

    def in_place(value):
        return pltpu.with_memory_space_constraint(value, pltpu.HBM)

    blocks = slot_rows(in_place(tokens), in_place(seq_row), in_place(modulation), bags, capacity)
    weights = chip_weights(in_place(w_qkv), head_count * HD)
    blocks = [block if k == 0 else swap(block, dz=k) for k, block in enumerate(blocks)]
    half = round_up(capacity, 32) // 2
    queries, pieces = [], []
    for k, block in enumerate(blocks):
        if across == 2 and along == 2:
            from_x, from_y = swap(block, dx=1), swap(block, dy=1)
            upper, lower = swap(from_x[:half], dy=1), swap(from_y[half:], dx=1)
            parts = [block, from_y, from_x, upper, lower]
        else:
            parts = [swap(block, dx=j // along, dy=j % along) if j else block for j in range(chips)]
        groups = [parts]
        if k == bags - 1 and len(parts) > chips:
            groups = [parts[: chips - 1], parts[chips - 1 :]]
        queries.append([])
        for group in groups:
            query, kv = project(group, weights, head_count)
            queries[k].append(query)
            pieces += [kv, swap(kv, core=1)]
    mixed = [None] * bags
    rounds = [[bags - 1, 0], list(range(1, bags - 1))] if bags > 2 else [list(range(bags))]

    def exchange(index):
        shares = []
        for j in range(chips):
            share = jnp.stack([mixed[k][j] for k in rounds[index]])
            shares.append(swap(share, dx=j // along, dy=j % along) if j else share)
        return shares

    for k in reversed(range(bags)):
        halves = 1
        mixed[k] = []
        for index in range(halves):
            part, kv = attend(queries[k], pieces, chips, capacity, index, halves)
            pieces = [kv]
            part = swap(part, dz=k) if k else part
            mixed[k] += [part[j] for j in range(part.shape[0])]
    shares = [exchange(index) for index in range(len(rounds))]
    done = []
    for index in range(len(rounds)):
        done.append(
            finish(
                tokens, seq_row, modulation, shares[index], done, rounds, index, w_out, w_fc1, w_fc2, capacity
            )
        )
    return done[-1]


def solution(mesh):
    placed = (P(("bag", "sp"), None), P(("bag", "sp")), P(), P(), P(), P(), P())
    return jax.shard_map(
        layer, mesh=mesh, in_specs=placed, out_specs=P(("bag", "sp"), None), check_vma=False
    )
```

```python
import functools
import math

import jax
import jax.numpy as jnp
from jax import lax
from jax.experimental import pallas as pl
from jax.experimental.pallas import tpu as pltpu
from jax.sharding import PartitionSpec as P


HD = 72
SEQ_BAG = 1
LANE = 128
EPS = 1e-06
HUGE = 1e30
AXES = ("bag", "sp")
BF16, F32 = jnp.bfloat16, jnp.float32


def vmem():
    return pl.BlockSpec(memory_space=pltpu.VMEM)


def hbm():
    return pl.BlockSpec(memory_space=pltpu.HBM)


def limit(mebibytes):
    return pltpu.CompilerParams(vmem_limit_bytes=mebibytes << 20)


def coordinates():
    along = lax.axis_size("sp") // lax.axis_size("bag")
    bag, sp = lax.axis_index("bag"), lax.axis_index("sp")
    return lax.div(sp, along), lax.div(bag, 2) * along + lax.rem(sp, along)


def layer_norm(values):
    center = values - jnp.mean(values, axis=-1, keepdims=True)
    spread = jnp.mean(center * center, axis=-1, keepdims=True)
    return center * lax.rsqrt(spread + EPS)


def to_column(row):
    n = row.shape[1]
    diagonal = lax.broadcasted_iota(jnp.int32, (n, n), 0) == lax.broadcasted_iota(jnp.int32, (n, n), 1)
    return jnp.sum(jnp.where(diagonal, jnp.broadcast_to(row, (n, n)), 0.0), axis=1, keepdims=True)


def slot_of_row(bag_row, capacity):
    n = bag_row.shape[1]
    earlier = lax.broadcasted_iota(jnp.int32, (n, n), 0) < lax.broadcasted_iota(jnp.int32, (n, n), 1)
    same = jnp.broadcast_to(to_column(bag_row), (n, n)) == jnp.broadcast_to(bag_row, (n, n))
    rank = jnp.sum(jnp.where(same & earlier, 1.0, 0.0), axis=0, keepdims=True)
    return (bag_row * capacity + rank).astype(jnp.int32)


def round_up(value, unit):
    return -(-value // unit) * unit


def window_base(start, total, wide):
    aligned, last = start // LANE * LANE, total - wide
    return min(aligned, last) if isinstance(start, int) else jnp.minimum(aligned, last)


def slot_kernel(capacity, tokens_ref, seq_ref, mod_ref, *out_refs):
    me, _ = coordinates()
    row_count, width = tokens_ref.shape
    block_count = len(out_refs)
    bag_row = ((seq_ref[...] // SEQ_BAG) ^ me).astype(F32)
    position = slot_of_row(bag_row, capacity)
    slot_ids = lax.broadcasted_iota(jnp.int32, (block_count * capacity, row_count), 0)
    pick = jnp.where(slot_ids == position, 1.0, 0.0)
    filled = jnp.sum(pick, axis=1, keepdims=True)
    rows = jnp.dot(pick.astype(BF16), tokens_ref[...], preferred_element_type=F32)
    first = lax.broadcasted_iota(jnp.int32, (capacity, width), 1) == 0
    for block, out_ref in enumerate(out_refs):
        rows_of = slice(block * capacity, (block + 1) * capacity)
        shift, scale = [mod_ref[column, pl.ds(block ^ me, 1)] for column in (0, 1)]
        normed = layer_norm(rows[rows_of]) * (1.0 + scale) + shift
        normed = jnp.where(first & (filled[rows_of] < 0.5), HUGE, normed)
        out_ref[...] = normed.astype(BF16)


def slot_rows(tokens, seq_row, modulation, bag_count, capacity):
    width = tokens.shape[1]
    return pl.pallas_call(
        functools.partial(slot_kernel, capacity),
        in_specs=[vmem(), vmem(), vmem()],
        out_specs=[vmem()] * bag_count,
        out_shape=[jax.ShapeDtypeStruct((capacity, width), BF16)] * bag_count,
        compiler_params=limit(16),
        name="slot_rows",
    )(tokens, seq_row, modulation)


def weight_kernel(part, chips, w_ref, out_ref, window_ref, sem):
    _, here = coordinates()
    depth, wide = window_ref.shape[1:]
    total = w_ref.shape[1]
    copies = []
    for kind in range(3):
        base = pl.multiple_of(window_base(kind * (total // 3) + here * part, total, wide), LANE)
        copies.append(
            pltpu.make_async_copy(w_ref.at[:, pl.ds(base, wide)], window_ref.at[kind], sem.at[kind])
        )
    for copy in copies:
        copy.start()
    for copy in copies:
        copy.wait()
    for chip in range(chips):

        @pl.when(here == chip)
        def _():
            pieces = []
            for kind in range(3):
                start = kind * (total // 3) + chip * part
                shift = start - window_base(start, total, wide)
                pieces.append(window_ref[kind][:, shift : shift + part])
            filler = out_ref.shape[1] - 3 * part
            if filler:
                pieces.append(jnp.zeros((depth, filler), BF16))
            out_ref[...] = jnp.concatenate(pieces, axis=1)


def chip_weights(w_qkv, part):
    depth, total = w_qkv.shape
    wide = round_up(part + LANE - math.gcd(part, LANE), LANE)
    return pl.pallas_call(
        functools.partial(weight_kernel, part, total // 3 // part),
        in_specs=[hbm()],
        out_specs=vmem(),
        out_shape=jax.ShapeDtypeStruct((depth, round_up(3 * part, LANE)), BF16),
        scratch_shapes=[pltpu.VMEM((3, depth, wide), BF16), pltpu.SemaphoreType.DMA((3,))],
        cost_estimate=pl.CostEstimate(flops=10**9, bytes_accessed=10**7, transcendentals=0),
        compiler_params=limit(16),
        name="chip_weights",
    )(w_qkv)


def project_kernel(head_count, *refs):
    w_ref, (q_ref, kv_ref) = refs[-3], refs[-2:]
    rows = jnp.concatenate([ref[...] for ref in refs[:-3]], axis=0)
    size = rows.shape[0]
    factor = math.log2(math.e) / math.sqrt(HD)
    empty = rows[:, :1].astype(F32) > 0.5 * HUGE
    start = jnp.where(empty, 0.0, rows[:, :LANE].astype(F32)).astype(BF16)
    rows = jnp.concatenate([start, rows[:, LANE:]], axis=1)
    made = jnp.dot(rows, w_ref[...], preferred_element_type=F32)
    lane = lax.broadcasted_iota(jnp.int32, (size, LANE), 1)
    bias = jnp.where(empty, -HUGE, 0.0)
    for kind in range(3):
        for head in range(head_count):
            column = (kind * head_count + head) * HD
            base, shift = column // LANE * LANE, column % LANE
            wide = LANE if shift + HD <= LANE else 2 * LANE
            value = made[:, base : base + wide]
            if shift:
                value = pltpu.roll(value, wide - shift, axis=1)
            value = value[:, :LANE]
            if kind == 0:
                value, beside = value * factor, 1.0
            else:
                beside = bias if kind == 1 else 1.0
            value = jnp.where(lane < HD, value, jnp.where(lane == HD, beside, 0.0)).astype(BF16)
            if kind == 0:
                q_ref[head] = value
            else:
                kv_ref[kind - 1, head] = value


def project(parts, weights, head_count):
    size, depth = sum(part.shape[0] for part in parts), weights.shape[0]
    return pl.pallas_call(
        functools.partial(project_kernel, head_count),
        in_specs=[vmem()] * (len(parts) + 1),
        out_specs=[vmem(), vmem()],
        out_shape=[
            jax.ShapeDtypeStruct((head_count, size, LANE), BF16),
            jax.ShapeDtypeStruct((2, head_count, size, LANE), BF16),
        ],
        cost_estimate=pl.CostEstimate(
            flops=2 * size * depth * weights.shape[1], bytes_accessed=4 * size * depth, transcendentals=0
        ),
        compiler_params=limit(12),
        name="project",
    )(*parts, weights)


def packed_rows(capacity, width):
    whole = width // LANE
    rest = width - whole * LANE
    if rest == 0:
        return whole * capacity, 0, 0
    if capacity % 16:
        return (whole + 1) * capacity, rest, capacity
    groups = LANE // rest
    tiles = -(-(capacity // 16) // groups)
    return whole * capacity + tiles * 16, rest, 16


def pack(block, write):
    capacity, width = block.shape
    whole = width // LANE
    for tile in range(whole):
        write(tile * capacity, block[:, tile * LANE : (tile + 1) * LANE])
    _, rest, size = packed_rows(capacity, width)
    if rest == 0:
        return
    tail = block[:, whole * LANE :]
    groups = 1 if size == capacity else LANE // rest
    for first in range(0, capacity // size, groups):
        pieces = [
            tail[group * size : (group + 1) * size]
            for group in range(first, min(first + groups, capacity // size))
        ]
        filler = LANE - rest * len(pieces)
        if filler:
            pieces.append(jnp.zeros((size, filler), block.dtype))
        write(whole * capacity + first // groups * size, jnp.concatenate(pieces, axis=1))


def unpack(packed, capacity, width):
    whole = width // LANE
    columns = [packed[tile * capacity : (tile + 1) * capacity] for tile in range(whole)]
    _, rest, size = packed_rows(capacity, width)
    if rest:
        groups = 1 if size == capacity else LANE // rest
        pieces = []
        for group in range(capacity // size):
            top = whole * capacity + group // groups * size
            left = group % groups * rest
            pieces.append(packed[top : top + size, left : left + rest])
        columns.append(jnp.concatenate(pieces, axis=0))
    return jnp.concatenate(columns, axis=1)


def attend_kernel(chips, capacity, query_count, piece_count, *refs):
    queries, pieces = refs[:query_count], refs[query_count : query_count + piece_count]
    out_ref = refs[query_count + piece_count]
    if piece_count > 1:
        kv_ref = refs[-1]
        at = 0
        for ref in pieces:
            kv_ref[:, :, at : at + ref.shape[2]] = ref[...]
            at += ref.shape[2]
    else:
        kv_ref = pieces[0]
    nt = (((1,), (1,)), ((), ()))
    results = []
    for head in range(kv_ref.shape[1]):
        query = jnp.concatenate([ref[head] for ref in queries], axis=0)
        score = lax.dot_general(query, kv_ref[0, head], nt, preferred_element_type=F32)
        top = jnp.max(score, axis=1, keepdims=True)
        probs = jnp.exp2(score - top).astype(BF16)
        mixed = jnp.dot(probs, kv_ref[1, head], preferred_element_type=F32)
        results.append(mixed[:, :HD] / mixed[:, HD : HD + 1])
    rows = jnp.concatenate(results, axis=1).astype(BF16)
    for chip in range(chips):
        block = rows[chip * capacity : (chip + 1) * capacity]

        def write(first, value):
            out_ref[chip, first : first + value.shape[0]] = value

        pack(block, write)


def attend(queries, pieces, chips, capacity):
    head_count, rows = queries[0].shape[0], chips * capacity
    keys = sum(piece.shape[2] for piece in pieces)
    out_rows = packed_rows(capacity, head_count * HD)[0]
    out_shape = [jax.ShapeDtypeStruct((chips, out_rows, LANE), BF16)]
    if len(pieces) > 1:
        out_shape.append(jax.ShapeDtypeStruct((2, head_count, keys, LANE), BF16))
    made = pl.pallas_call(
        functools.partial(attend_kernel, chips, capacity, len(queries), len(pieces)),
        in_specs=[vmem()] * (len(queries) + len(pieces)),
        out_specs=[vmem()] * len(out_shape),
        out_shape=out_shape,
        cost_estimate=pl.CostEstimate(
            flops=4 * head_count * rows * keys * LANE,
            bytes_accessed=4 * head_count * keys * LANE,
            transcendentals=head_count * rows * keys,
        ),
        compiler_params=limit(24),
        name="attend",
    )(*queries, *pieces)
    return made[0], (made[1] if len(pieces) > 1 else pieces[0])


def finish_kernel(capacity, chips, rounds, index, tokens_ref, seq_ref, mod_ref, w_out, w_fc1, w_fc2, *refs):
    parts, earlier, out_ref, whole = refs[:chips], refs[chips:-2], refs[-2], refs[-1]
    members = rounds[index]
    row_count, width = tokens_ref.shape
    plane, here = coordinates()
    for chip, part in enumerate(parts):
        whole[here ^ chip] = part[...]
    position = slot_of_row(((seq_ref[...] // SEQ_BAG) ^ plane).astype(F32), capacity)

    def picks(bags):
        slot_ids = lax.broadcasted_iota(jnp.int32, (capacity, row_count), 0)
        blocks = [jnp.where(slot_ids + bag * capacity == position, 1.0, 0.0) for bag in bags]
        return jnp.concatenate(blocks, axis=0).astype(BF16)

    def per_slot(column):
        rows = [mod_ref[column, pl.ds(bag ^ plane, 1)] for bag in members]
        return jnp.concatenate([jnp.broadcast_to(row, (capacity, width)) for row in rows], axis=0)

    attended = jnp.concatenate(
        [
            jnp.concatenate(
                [unpack(whole[chip, at], capacity, width // chips) for chip in range(chips)], axis=1
            )
            for at in range(len(members))
        ],
        axis=0,
    )
    residual = jnp.dot(picks(members), tokens_ref[...], preferred_element_type=F32)
    branch = jnp.dot(attended, w_out[...], preferred_element_type=F32)
    hidden = (residual + per_slot(2) * branch).astype(BF16)
    normed = (layer_norm(hidden.astype(F32)) * (1.0 + per_slot(4)) + per_slot(3)).astype(BF16)
    active = jax.nn.gelu(jnp.dot(normed, w_fc1[...], preferred_element_type=F32), approximate=True)
    last = jnp.dot(active.astype(BF16), w_fc2[...], preferred_element_type=F32)
    slots = (hidden.astype(F32) + per_slot(5) * last).astype(BF16)
    if index < len(rounds) - 1:
        out_ref[...] = slots
        return
    slots = jnp.concatenate([ref[...] for ref in earlier] + [slots], axis=0)
    tn = (((0,), (0,)), ((), ()))
    pick = picks([bag for bags in rounds for bag in bags])
    out_ref[...] = lax.dot_general(pick, slots, tn, preferred_element_type=F32).astype(BF16)


def finish(tokens, seq_row, modulation, parts, earlier, rounds, index, w_out, w_fc1, w_fc2, capacity):
    chips, slot_count = len(parts), capacity * len(rounds[index])
    final = index == len(rounds) - 1
    width, depth = tokens.shape[1], w_fc1.shape[1]
    return pl.pallas_call(
        functools.partial(finish_kernel, capacity, chips, rounds, index),
        in_specs=[vmem()] * (6 + chips + len(earlier)),
        out_specs=vmem(),
        out_shape=jax.ShapeDtypeStruct(tokens.shape if final else (slot_count, width), BF16),
        scratch_shapes=[pltpu.VMEM((chips,) + parts[0].shape, BF16)],
        cost_estimate=pl.CostEstimate(
            flops=2 * slot_count * width * (width + 2 * depth),
            bytes_accessed=2 * width * (width + 2 * depth),
            transcendentals=slot_count * depth,
        ),
        compiler_params=limit(20),
        name="finish",
    )(tokens, seq_row, modulation, w_out, w_fc1, w_fc2, *parts, *earlier)


def layer(tokens, row_seq, modulation, w_qkv, w_out, w_fc1, w_fc2):
    bags, sp = lax.axis_size("bag"), lax.axis_size("sp")
    along, across, cores = sp // bags, bags // 2, 2
    chips = across * along
    row_count, width = tokens.shape
    capacity = row_count // bags * 5 // 4
    head_count = width // HD // chips

    def swap(value, dx=0, core=0, dz=0, dy=0):
        pairs = []
        for b in range(bags):
            for s in range(sp):
                b2 = ((b // cores) ^ dx) * cores + ((b % cores) ^ core)
                s2 = ((s // along) ^ dz) * along + ((s % along) ^ dy)
                pairs.append((b * sp + s, b2 * sp + s2))
        return lax.ppermute(value, AXES, pairs)

    seq_row = row_seq.reshape(1, row_count)
    modulation = jnp.transpose(modulation, (1, 0, 2))

    def in_place(value):
        return pltpu.with_memory_space_constraint(value, pltpu.HBM)

    blocks = slot_rows(in_place(tokens), in_place(seq_row), in_place(modulation), bags, capacity)
    weights = chip_weights(in_place(w_qkv), head_count * HD)
    blocks = [block if k == 0 else swap(block, dz=k) for k, block in enumerate(blocks)]
    half = round_up(capacity, 32) // 2
    queries, pieces = [], []
    for k, block in enumerate(blocks):
        if across == 2 and along == 2:
            from_x, from_y = swap(block, dx=1), swap(block, dy=1)
            upper, lower = swap(from_x[:half], dy=1), swap(from_y[half:], dx=1)
            parts = [block, from_y, from_x, upper, lower]
        else:
            parts = [swap(block, dx=j // along, dy=j % along) if j else block for j in range(chips)]
        groups = [parts]
        if k == bags - 1 and len(parts) > chips:
            groups = [parts[: chips - 1], parts[chips - 1 :]]
        queries.append([])
        for group in groups:
            query, kv = project(group, weights, head_count)
            queries[k].append(query)
            pieces += [kv, swap(kv, core=1)]
    mixed = [None] * bags
    rounds = [[bags - 1, 0], list(range(1, bags - 1))] if bags > 2 else [list(range(bags))]

    def exchange(index):
        shares = []
        for j in range(chips):
            share = jnp.stack([mixed[k][j] for k in rounds[index]])
            shares.append(swap(share, dx=j // along, dy=j % along) if j else share)
        return shares

    for k in reversed(range(1, bags)):
        asked = queries[k] if k > 1 else queries[1] + queries[0]
        part, kv = attend(asked, pieces, chips if k > 1 else 2 * chips, capacity)
        pieces = [kv]
        part = [part[j] for j in range(part.shape[0])]
        if k == 1:
            mixed[0] = part[chips:]
        away = swap(jnp.stack(part[:chips]), dz=k)
        mixed[k] = [away[j] for j in range(chips)]
    shares = [exchange(index) for index in range(len(rounds))]
    done = []
    for index in range(len(rounds)):
        done.append(
            finish(
                tokens, seq_row, modulation, shares[index], done, rounds, index, w_out, w_fc1, w_fc2, capacity
            )
        )
    return done[-1]


def solution(mesh):
    placed = (P(("bag", "sp"), None), P(("bag", "sp")), P(), P(), P(), P(), P())
    return jax.shard_map(
        layer, mesh=mesh, in_specs=placed, out_specs=P(("bag", "sp"), None), check_vma=False
    )
```

```python
import functools
import math

import jax
import jax.numpy as jnp
from jax import lax
from jax.experimental import pallas as pl
from jax.experimental.pallas import tpu as pltpu
from jax.sharding import PartitionSpec as P


HD = 72
SEQ_BAG = 1
LANE = 128
EPS = 1e-06
HUGE = 1e30
AXES = ("bag", "sp")
BF16, F32 = jnp.bfloat16, jnp.float32


def vmem():
    return pl.BlockSpec(memory_space=pltpu.VMEM)


def hbm():
    return pl.BlockSpec(memory_space=pltpu.HBM)


def limit(mebibytes):
    return pltpu.CompilerParams(vmem_limit_bytes=mebibytes << 20)


def coordinates():
    along = lax.axis_size("sp") // lax.axis_size("bag")
    bag, sp = lax.axis_index("bag"), lax.axis_index("sp")
    return lax.div(sp, along), lax.div(bag, 2) * along + lax.rem(sp, along)


def layer_norm(values):
    center = values - jnp.mean(values, axis=-1, keepdims=True)
    spread = jnp.mean(center * center, axis=-1, keepdims=True)
    return center * lax.rsqrt(spread + EPS)


def to_column(row):
    n = row.shape[1]
    diagonal = lax.broadcasted_iota(jnp.int32, (n, n), 0) == lax.broadcasted_iota(jnp.int32, (n, n), 1)
    return jnp.sum(jnp.where(diagonal, jnp.broadcast_to(row, (n, n)), 0.0), axis=1, keepdims=True)


def slot_of_row(bag_row, capacity):
    n = bag_row.shape[1]
    earlier = lax.broadcasted_iota(jnp.int32, (n, n), 0) < lax.broadcasted_iota(jnp.int32, (n, n), 1)
    same = jnp.broadcast_to(to_column(bag_row), (n, n)) == jnp.broadcast_to(bag_row, (n, n))
    rank = jnp.sum(jnp.where(same & earlier, 1.0, 0.0), axis=0, keepdims=True)
    return (bag_row * capacity + rank).astype(jnp.int32)


def round_up(value, unit):
    return -(-value // unit) * unit


def window_base(start, total, wide):
    aligned, last = start // LANE * LANE, total - wide
    return min(aligned, last) if isinstance(start, int) else jnp.minimum(aligned, last)


def slot_kernel(capacity, tokens_ref, seq_ref, mod_ref, raw_ref, pick_ref, *out_refs):
    me, _ = coordinates()
    row_count, width = tokens_ref.shape
    block_count = len(out_refs)
    bag_row = ((seq_ref[...] // SEQ_BAG) ^ me).astype(F32)
    position = slot_of_row(bag_row, capacity)
    slot_ids = lax.broadcasted_iota(jnp.int32, (block_count * capacity, row_count), 0)
    pick = jnp.where(slot_ids == position, 1.0, 0.0)
    filled = jnp.sum(pick, axis=1, keepdims=True)
    rows = jnp.dot(pick.astype(BF16), tokens_ref[...], preferred_element_type=F32)
    pick_ref[...] = pick.astype(BF16)
    raw_ref[...] = rows.astype(BF16)
    first = lax.broadcasted_iota(jnp.int32, (capacity, width), 1) == 0
    for block, out_ref in enumerate(out_refs):
        rows_of = slice(block * capacity, (block + 1) * capacity)
        shift, scale = [mod_ref[column, pl.ds(block ^ me, 1)] for column in (0, 1)]
        normed = layer_norm(rows[rows_of]) * (1.0 + scale) + shift
        normed = jnp.where(first & (filled[rows_of] < 0.5), HUGE, normed)
        out_ref[...] = normed.astype(BF16)


def slot_rows(tokens, seq_row, modulation, bag_count, capacity):
    row_count, width = tokens.shape
    slot_count = bag_count * capacity
    raw, pick, *blocks = pl.pallas_call(
        functools.partial(slot_kernel, capacity),
        in_specs=[vmem(), vmem(), vmem()],
        out_specs=[vmem()] * (2 + bag_count),
        out_shape=[
            jax.ShapeDtypeStruct((slot_count, width), BF16),
            jax.ShapeDtypeStruct((slot_count, row_count), BF16),
        ]
        + [jax.ShapeDtypeStruct((capacity, width), BF16)] * bag_count,
        compiler_params=limit(16),
        name="slot_rows",
    )(tokens, seq_row, modulation)
    return raw, pick, blocks


def weight_kernel(part, chips, w_ref, out_ref, window_ref, sem):
    _, here = coordinates()
    depth, wide = window_ref.shape[1:]
    total = w_ref.shape[1]
    copies = []
    for kind in range(3):
        base = pl.multiple_of(window_base(kind * (total // 3) + here * part, total, wide), LANE)
        copies.append(
            pltpu.make_async_copy(w_ref.at[:, pl.ds(base, wide)], window_ref.at[kind], sem.at[kind])
        )
    for copy in copies:
        copy.start()
    for copy in copies:
        copy.wait()
    for chip in range(chips):

        @pl.when(here == chip)
        def _():
            pieces = []
            for kind in range(3):
                start = kind * (total // 3) + chip * part
                shift = start - window_base(start, total, wide)
                pieces.append(window_ref[kind][:, shift : shift + part])
            filler = out_ref.shape[1] - 3 * part
            if filler:
                pieces.append(jnp.zeros((depth, filler), BF16))
            out_ref[...] = jnp.concatenate(pieces, axis=1)


def chip_weights(w_qkv, part):
    depth, total = w_qkv.shape
    wide = round_up(part + LANE - math.gcd(part, LANE), LANE)
    return pl.pallas_call(
        functools.partial(weight_kernel, part, total // 3 // part),
        in_specs=[hbm()],
        out_specs=vmem(),
        out_shape=jax.ShapeDtypeStruct((depth, round_up(3 * part, LANE)), BF16),
        scratch_shapes=[pltpu.VMEM((3, depth, wide), BF16), pltpu.SemaphoreType.DMA((3,))],
        cost_estimate=pl.CostEstimate(flops=10**9, bytes_accessed=10**7, transcendentals=0),
        compiler_params=limit(16),
        name="chip_weights",
    )(w_qkv)


def project_kernel(head_count, *refs):
    w_ref, (q_ref, kv_ref) = refs[-3], refs[-2:]
    rows = jnp.concatenate([ref[...] for ref in refs[:-3]], axis=0)
    size = rows.shape[0]
    factor = math.log2(math.e) / math.sqrt(HD)
    empty = rows[:, :1].astype(F32) > 0.5 * HUGE
    start = jnp.where(empty, 0.0, rows[:, :LANE].astype(F32)).astype(BF16)
    rows = jnp.concatenate([start, rows[:, LANE:]], axis=1)
    made = jnp.dot(rows, w_ref[...], preferred_element_type=F32)
    lane = lax.broadcasted_iota(jnp.int32, (size, LANE), 1)
    bias = jnp.where(empty, -HUGE, 0.0)
    for kind in range(3):
        for head in range(head_count):
            column = (kind * head_count + head) * HD
            base, shift = column // LANE * LANE, column % LANE
            wide = LANE if shift + HD <= LANE else 2 * LANE
            value = made[:, base : base + wide]
            if shift:
                value = pltpu.roll(value, wide - shift, axis=1)
            value = value[:, :LANE]
            if kind == 0:
                value, beside = value * factor, 1.0
            else:
                beside = bias if kind == 1 else 1.0
            value = jnp.where(lane < HD, value, jnp.where(lane == HD, beside, 0.0)).astype(BF16)
            if kind == 0:
                q_ref[head] = value
            else:
                kv_ref[kind - 1, head] = value


def project(parts, weights, head_count):
    size, depth = sum(part.shape[0] for part in parts), weights.shape[0]
    return pl.pallas_call(
        functools.partial(project_kernel, head_count),
        in_specs=[vmem()] * (len(parts) + 1),
        out_specs=[vmem(), vmem()],
        out_shape=[
            jax.ShapeDtypeStruct((head_count, size, LANE), BF16),
            jax.ShapeDtypeStruct((2, head_count, size, LANE), BF16),
        ],
        cost_estimate=pl.CostEstimate(
            flops=2 * size * depth * weights.shape[1], bytes_accessed=4 * size * depth, transcendentals=0
        ),
        compiler_params=limit(12),
        name="project",
    )(*parts, weights)


def packed_rows(capacity, width):
    whole = width // LANE
    rest = width - whole * LANE
    if rest == 0:
        return whole * capacity, 0, 0
    if capacity % 16:
        return (whole + 1) * capacity, rest, capacity
    groups = LANE // rest
    tiles = -(-(capacity // 16) // groups)
    return whole * capacity + tiles * 16, rest, 16


def pack(block, write):
    capacity, width = block.shape
    whole = width // LANE
    for tile in range(whole):
        write(tile * capacity, block[:, tile * LANE : (tile + 1) * LANE])
    _, rest, size = packed_rows(capacity, width)
    if rest == 0:
        return
    tail = block[:, whole * LANE :]
    groups = 1 if size == capacity else LANE // rest
    for first in range(0, capacity // size, groups):
        pieces = [
            tail[group * size : (group + 1) * size]
            for group in range(first, min(first + groups, capacity // size))
        ]
        filler = LANE - rest * len(pieces)
        if filler:
            pieces.append(jnp.zeros((size, filler), block.dtype))
        write(whole * capacity + first // groups * size, jnp.concatenate(pieces, axis=1))


def unpack(packed, capacity, width):
    whole = width // LANE
    columns = [packed[tile * capacity : (tile + 1) * capacity] for tile in range(whole)]
    _, rest, size = packed_rows(capacity, width)
    if rest:
        groups = 1 if size == capacity else LANE // rest
        pieces = []
        for group in range(capacity // size):
            top = whole * capacity + group // groups * size
            left = group % groups * rest
            pieces.append(packed[top : top + size, left : left + rest])
        columns.append(jnp.concatenate(pieces, axis=0))
    return jnp.concatenate(columns, axis=1)


def attend_kernel(chips, capacity, query_count, piece_count, *refs):
    queries, pieces = refs[:query_count], refs[query_count : query_count + piece_count]
    out_ref = refs[query_count + piece_count]
    if piece_count > 1:
        kv_ref = refs[-1]
        at = 0
        for ref in pieces:
            kv_ref[:, :, at : at + ref.shape[2]] = ref[...]
            at += ref.shape[2]
    else:
        kv_ref = pieces[0]
    nt = (((1,), (1,)), ((), ()))
    results = []
    for head in range(kv_ref.shape[1]):
        query = jnp.concatenate([ref[head] for ref in queries], axis=0)
        score = lax.dot_general(query, kv_ref[0, head], nt, preferred_element_type=F32)
        top = jnp.max(score, axis=1, keepdims=True)
        probs = jnp.exp2(score - top).astype(BF16)
        mixed = jnp.dot(probs, kv_ref[1, head], preferred_element_type=F32)
        results.append(mixed[:, :HD] / mixed[:, HD : HD + 1])
    rows = jnp.concatenate(results, axis=1).astype(BF16)
    for chip in range(chips):
        block = rows[chip * capacity : (chip + 1) * capacity]

        def write(first, value):
            out_ref[chip, first : first + value.shape[0]] = value

        pack(block, write)


def attend(queries, pieces, chips, capacity):
    head_count, rows = queries[0].shape[0], chips * capacity
    keys = sum(piece.shape[2] for piece in pieces)
    out_rows = packed_rows(capacity, head_count * HD)[0]
    out_shape = [jax.ShapeDtypeStruct((chips, out_rows, LANE), BF16)]
    if len(pieces) > 1:
        out_shape.append(jax.ShapeDtypeStruct((2, head_count, keys, LANE), BF16))
    made = pl.pallas_call(
        functools.partial(attend_kernel, chips, capacity, len(queries), len(pieces)),
        in_specs=[vmem()] * (len(queries) + len(pieces)),
        out_specs=[vmem()] * len(out_shape),
        out_shape=out_shape,
        cost_estimate=pl.CostEstimate(
            flops=4 * head_count * rows * keys * LANE,
            bytes_accessed=4 * head_count * keys * LANE,
            transcendentals=head_count * rows * keys,
        ),
        compiler_params=limit(24),
        name="attend",
    )(*queries, *pieces)
    return made[0], (made[1] if len(pieces) > 1 else pieces[0])


def finish_kernel(capacity, chips, rounds, index, raw_ref, pick_ref, mod_ref, w_out, w_fc1, w_fc2, *refs):
    parts, earlier, out_ref, whole = refs[:chips], refs[chips:-2], refs[-2], refs[-1]
    members = rounds[index]
    width = raw_ref.shape[1]
    plane, here = coordinates()
    for chip, part in enumerate(parts):
        whole[here ^ chip] = part[...]

    def per_slot(column):
        rows = [mod_ref[column, pl.ds(bag ^ plane, 1)] for bag in members]
        return jnp.concatenate([jnp.broadcast_to(row, (capacity, width)) for row in rows], axis=0)

    attended = jnp.concatenate(
        [
            jnp.concatenate(
                [unpack(whole[chip, at], capacity, width // chips) for chip in range(chips)], axis=1
            )
            for at in range(len(members))
        ],
        axis=0,
    )
    residual = jnp.concatenate(
        [raw_ref[bag * capacity : (bag + 1) * capacity] for bag in members], axis=0
    ).astype(F32)
    branch = jnp.dot(attended, w_out[...], preferred_element_type=F32)
    hidden = (residual + per_slot(2) * branch).astype(BF16)
    normed = (layer_norm(hidden.astype(F32)) * (1.0 + per_slot(4)) + per_slot(3)).astype(BF16)
    active = jax.nn.gelu(jnp.dot(normed, w_fc1[...], preferred_element_type=F32), approximate=True)
    last = jnp.dot(active.astype(BF16), w_fc2[...], preferred_element_type=F32)
    slots = (hidden.astype(F32) + per_slot(5) * last).astype(BF16)
    if index < len(rounds) - 1:
        out_ref[...] = slots
        return
    blocks = {}
    for bags, value in zip(rounds, [ref[...] for ref in earlier] + [slots]):
        for at, bag in enumerate(bags):
            blocks[bag] = value[at * capacity : (at + 1) * capacity]
    slots = jnp.concatenate([blocks[bag] for bag in range(len(blocks))], axis=0)
    tn = (((0,), (0,)), ((), ()))
    out_ref[...] = lax.dot_general(pick_ref[...], slots, tn, preferred_element_type=F32).astype(BF16)


def finish(raw, pick, modulation, parts, earlier, rounds, index, w_out, w_fc1, w_fc2, capacity):
    chips, slot_count = len(parts), capacity * len(rounds[index])
    final = index == len(rounds) - 1
    width, depth, row_count = raw.shape[1], w_fc1.shape[1], pick.shape[1]
    return pl.pallas_call(
        functools.partial(finish_kernel, capacity, chips, rounds, index),
        in_specs=[vmem()] * (6 + chips + len(earlier)),
        out_specs=vmem(),
        out_shape=jax.ShapeDtypeStruct((row_count if final else slot_count, width), BF16),
        scratch_shapes=[pltpu.VMEM((chips,) + parts[0].shape, BF16)],
        cost_estimate=pl.CostEstimate(
            flops=2 * slot_count * width * (width + 2 * depth),
            bytes_accessed=2 * width * (width + 2 * depth),
            transcendentals=slot_count * depth,
        ),
        compiler_params=limit(20),
        name="finish",
    )(raw, pick, modulation, w_out, w_fc1, w_fc2, *parts, *earlier)


def attended_together(bags):
    middle = list(reversed(range(1, bags - 1)))
    return [[bags - 1]] + [middle[at : at + 2] for at in range(0, len(middle), 2)] + [[0]]


def layer(tokens, row_seq, modulation, w_qkv, w_out, w_fc1, w_fc2):
    bags, sp = lax.axis_size("bag"), lax.axis_size("sp")
    along, across, cores = sp // bags, bags // 2, 2
    chips = across * along
    row_count, width = tokens.shape
    capacity = row_count // bags * 5 // 4
    head_count = width // HD // chips

    def swap(value, dx=0, core=0, dz=0, dy=0):
        pairs = []
        for b in range(bags):
            for s in range(sp):
                b2 = ((b // cores) ^ dx) * cores + ((b % cores) ^ core)
                s2 = ((s // along) ^ dz) * along + ((s % along) ^ dy)
                pairs.append((b * sp + s, b2 * sp + s2))
        return lax.ppermute(value, AXES, pairs)

    seq_row = row_seq.reshape(1, row_count)
    modulation = jnp.transpose(modulation, (1, 0, 2))

    def in_place(value):
        return pltpu.with_memory_space_constraint(value, pltpu.HBM)

    inputs = [in_place(value) for value in (tokens, seq_row, modulation)]
    raw, pick, blocks = slot_rows(*inputs, bags, capacity)
    weights = chip_weights(in_place(w_qkv), head_count * HD)
    blocks = [block if k == 0 else swap(block, dz=k) for k, block in enumerate(blocks)]
    half = round_up(capacity, 32) // 2
    queries, pieces = [], []
    for k, block in enumerate(blocks):
        if across == 2 and along == 2:
            from_x, from_y = swap(block, dx=1), swap(block, dy=1)
            upper, lower = swap(from_x[:half], dy=1), swap(from_y[half:], dx=1)
            parts = [block, from_y, from_x, upper, lower]
        else:
            parts = [swap(block, dx=j // along, dy=j % along) if j else block for j in range(chips)]
        groups = [parts]
        if k == bags - 1 and len(parts) > chips:
            groups = [parts[: chips - 1], parts[chips - 1 :]]
        queries.append([])
        for group in groups:
            query, kv = project(group, weights, head_count)
            queries[k].append(query)
            pieces += [kv, swap(kv, core=1)]
    mixed = [None] * bags
    rounds = [[bags - 1, 0], list(range(1, bags - 1))] if bags > 2 else [list(range(bags))]

    def exchange(index):
        shares = []
        for j in range(chips):
            share = jnp.stack([mixed[k][j] for k in rounds[index]])
            shares.append(swap(share, dx=j // along, dy=j % along) if j else share)
        return shares

    for members in attended_together(bags):
        asked = [query for k in members for query in queries[k]]
        part, kv = attend(asked, pieces, chips * len(members), capacity)
        pieces = [kv]
        for at, k in enumerate(members):
            share = part[at * chips : (at + 1) * chips]
            share = swap(share, dz=k) if k else share
            mixed[k] = [share[j] for j in range(chips)]
    shares = [exchange(index) for index in range(len(rounds))]
    done = []
    for index in range(len(rounds)):
        done.append(
            finish(
                raw, pick, modulation, shares[index], done, rounds, index, w_out, w_fc1, w_fc2, capacity
            )
        )
    return done[-1]


def solution(mesh):
    placed = (P(("bag", "sp"), None), P(("bag", "sp")), P(), P(), P(), P(), P())
    return jax.shard_map(
        layer, mesh=mesh, in_specs=placed, out_specs=P(("bag", "sp"), None), check_vma=False
    )
```

```python
import functools
import math

import jax
import jax.numpy as jnp
from jax import lax
from jax.experimental import pallas as pl
from jax.experimental.pallas import tpu as pltpu
from jax.sharding import PartitionSpec as P


HD = 72
SEQ_BAG = 1
LANE = 128
EPS = 1e-06
HUGE = 1e30
AXES = ("bag", "sp")
BF16, F32 = jnp.bfloat16, jnp.float32


def vmem():
    return pl.BlockSpec(memory_space=pltpu.VMEM)


def hbm():
    return pl.BlockSpec(memory_space=pltpu.HBM)


def limit(mebibytes):
    return pltpu.CompilerParams(vmem_limit_bytes=mebibytes << 20)


def coordinates():
    along = lax.axis_size("sp") // lax.axis_size("bag")
    bag, sp = lax.axis_index("bag"), lax.axis_index("sp")
    return lax.div(sp, along), lax.div(bag, 2) * along + lax.rem(sp, along)


def layer_norm(values):
    center = values - jnp.mean(values, axis=-1, keepdims=True)
    spread = jnp.mean(center * center, axis=-1, keepdims=True)
    return center * lax.rsqrt(spread + EPS)


def to_column(row):
    n = row.shape[1]
    diagonal = lax.broadcasted_iota(jnp.int32, (n, n), 0) == lax.broadcasted_iota(jnp.int32, (n, n), 1)
    return jnp.sum(jnp.where(diagonal, jnp.broadcast_to(row, (n, n)), 0.0), axis=1, keepdims=True)


def slot_of_row(bag_row, capacity):
    n = bag_row.shape[1]
    earlier = lax.broadcasted_iota(jnp.int32, (n, n), 0) < lax.broadcasted_iota(jnp.int32, (n, n), 1)
    same = jnp.broadcast_to(to_column(bag_row), (n, n)) == jnp.broadcast_to(bag_row, (n, n))
    rank = jnp.sum(jnp.where(same & earlier, 1.0, 0.0), axis=0, keepdims=True)
    return (bag_row * capacity + rank).astype(jnp.int32)


def round_up(value, unit):
    return -(-value // unit) * unit


def window_base(start, total, wide):
    aligned, last = start // LANE * LANE, total - wide
    return min(aligned, last) if isinstance(start, int) else jnp.minimum(aligned, last)


def slot_kernel(capacity, tokens_ref, seq_ref, mod_ref, raw_ref, pick_ref, *out_refs):
    me, _ = coordinates()
    row_count, width = tokens_ref.shape
    block_count = len(out_refs)
    bag_row = ((seq_ref[...] // SEQ_BAG) ^ me).astype(F32)
    position = slot_of_row(bag_row, capacity)
    slot_ids = lax.broadcasted_iota(jnp.int32, (block_count * capacity, row_count), 0)
    pick = jnp.where(slot_ids == position, 1.0, 0.0)
    filled = jnp.sum(pick, axis=1, keepdims=True)
    rows = jnp.dot(pick.astype(BF16), tokens_ref[...], preferred_element_type=F32)
    pick_ref[...] = pick.astype(BF16)
    raw_ref[...] = rows.astype(BF16)
    first = lax.broadcasted_iota(jnp.int32, (capacity, width), 1) == 0
    for block, out_ref in enumerate(out_refs):
        rows_of = slice(block * capacity, (block + 1) * capacity)
        shift, scale = [mod_ref[column, pl.ds(block ^ me, 1)] for column in (0, 1)]
        normed = layer_norm(rows[rows_of]) * (1.0 + scale) + shift
        normed = jnp.where(first & (filled[rows_of] < 0.5), HUGE, normed)
        out_ref[...] = normed.astype(BF16)


def slot_rows(tokens, seq_row, modulation, bag_count, capacity):
    row_count, width = tokens.shape
    slot_count = bag_count * capacity
    raw, pick, *blocks = pl.pallas_call(
        functools.partial(slot_kernel, capacity),
        in_specs=[vmem(), vmem(), vmem()],
        out_specs=[vmem()] * (2 + bag_count),
        out_shape=[
            jax.ShapeDtypeStruct((slot_count, width), BF16),
            jax.ShapeDtypeStruct((slot_count, row_count), BF16),
        ]
        + [jax.ShapeDtypeStruct((capacity, width), BF16)] * bag_count,
        compiler_params=limit(16),
        name="slot_rows",
    )(tokens, seq_row, modulation)
    return raw, pick, blocks


def weight_kernel(part, chips, w_ref, out_ref, window_ref, sem):
    _, here = coordinates()
    depth, wide = window_ref.shape[1:]
    total = w_ref.shape[1]
    copies = []
    for kind in range(3):
        base = pl.multiple_of(window_base(kind * (total // 3) + here * part, total, wide), LANE)
        copies.append(
            pltpu.make_async_copy(w_ref.at[:, pl.ds(base, wide)], window_ref.at[kind], sem.at[kind])
        )
    for copy in copies:
        copy.start()
    for copy in copies:
        copy.wait()
    for chip in range(chips):

        @pl.when(here == chip)
        def _():
            pieces = []
            for kind in range(3):
                start = kind * (total // 3) + chip * part
                shift = start - window_base(start, total, wide)
                pieces.append(window_ref[kind][:, shift : shift + part])
            filler = out_ref.shape[1] - 3 * part
            if filler:
                pieces.append(jnp.zeros((depth, filler), BF16))
            out_ref[...] = jnp.concatenate(pieces, axis=1)


def chip_weights(w_qkv, part):
    depth, total = w_qkv.shape
    wide = round_up(part + LANE - math.gcd(part, LANE), LANE)
    return pl.pallas_call(
        functools.partial(weight_kernel, part, total // 3 // part),
        in_specs=[hbm()],
        out_specs=vmem(),
        out_shape=jax.ShapeDtypeStruct((depth, round_up(3 * part, LANE)), BF16),
        scratch_shapes=[pltpu.VMEM((3, depth, wide), BF16), pltpu.SemaphoreType.DMA((3,))],
        cost_estimate=pl.CostEstimate(flops=10**9, bytes_accessed=10**7, transcendentals=0),
        compiler_params=limit(16),
        name="chip_weights",
    )(w_qkv)


def project_kernel(head_count, *refs):
    w_ref, (q_ref, kv_ref) = refs[-3], refs[-2:]
    rows = jnp.concatenate([ref[...] for ref in refs[:-3]], axis=0)
    size = rows.shape[0]
    factor = math.log2(math.e) / math.sqrt(HD)
    empty = rows[:, :1].astype(F32) > 0.5 * HUGE
    start = jnp.where(empty, 0.0, rows[:, :LANE].astype(F32)).astype(BF16)
    rows = jnp.concatenate([start, rows[:, LANE:]], axis=1)
    made = jnp.dot(rows, w_ref[...], preferred_element_type=F32)
    lane = lax.broadcasted_iota(jnp.int32, (size, LANE), 1)
    bias = jnp.where(empty, -HUGE, 0.0)
    for kind in range(3):
        for head in range(head_count):
            column = (kind * head_count + head) * HD
            base, shift = column // LANE * LANE, column % LANE
            wide = LANE if shift + HD <= LANE else 2 * LANE
            value = made[:, base : base + wide]
            if shift:
                value = pltpu.roll(value, wide - shift, axis=1)
            value = value[:, :LANE]
            if kind == 0:
                value, beside = value * factor, 1.0
            else:
                beside = bias if kind == 1 else 1.0
            value = jnp.where(lane < HD, value, jnp.where(lane == HD, beside, 0.0)).astype(BF16)
            if kind == 0:
                q_ref[head] = value
            else:
                kv_ref[kind - 1, head] = value


def project(parts, weights, head_count):
    size, depth = sum(part.shape[0] for part in parts), weights.shape[0]
    return pl.pallas_call(
        functools.partial(project_kernel, head_count),
        in_specs=[vmem()] * (len(parts) + 1),
        out_specs=[vmem(), vmem()],
        out_shape=[
            jax.ShapeDtypeStruct((head_count, size, LANE), BF16),
            jax.ShapeDtypeStruct((2, head_count, size, LANE), BF16),
        ],
        cost_estimate=pl.CostEstimate(
            flops=2 * size * depth * weights.shape[1], bytes_accessed=4 * size * depth, transcendentals=0
        ),
        compiler_params=limit(12),
        name="project",
    )(*parts, weights)


def packed_rows(capacity, width):
    whole = width // LANE
    rest = width - whole * LANE
    if rest == 0:
        return whole * capacity, 0, 0
    if capacity % 16:
        return (whole + 1) * capacity, rest, capacity
    groups = LANE // rest
    tiles = -(-(capacity // 16) // groups)
    return whole * capacity + tiles * 16, rest, 16


def pack(block, write):
    capacity, width = block.shape
    whole = width // LANE
    for tile in range(whole):
        write(tile * capacity, block[:, tile * LANE : (tile + 1) * LANE])
    _, rest, size = packed_rows(capacity, width)
    if rest == 0:
        return
    tail = block[:, whole * LANE :]
    groups = 1 if size == capacity else LANE // rest
    for first in range(0, capacity // size, groups):
        pieces = [
            tail[group * size : (group + 1) * size]
            for group in range(first, min(first + groups, capacity // size))
        ]
        filler = LANE - rest * len(pieces)
        if filler:
            pieces.append(jnp.zeros((size, filler), block.dtype))
        write(whole * capacity + first // groups * size, jnp.concatenate(pieces, axis=1))


def unpack(packed, capacity, width):
    whole = width // LANE
    columns = [packed[tile * capacity : (tile + 1) * capacity] for tile in range(whole)]
    _, rest, size = packed_rows(capacity, width)
    if rest:
        groups = 1 if size == capacity else LANE // rest
        pieces = []
        for group in range(capacity // size):
            top = whole * capacity + group // groups * size
            left = group % groups * rest
            pieces.append(packed[top : top + size, left : left + rest])
        columns.append(jnp.concatenate(pieces, axis=0))
    return jnp.concatenate(columns, axis=1)


def attend_kernel(chips, capacity, query_count, piece_count, *refs):
    queries, pieces = refs[:query_count], refs[query_count : query_count + piece_count]
    out_ref = refs[query_count + piece_count]
    if piece_count > 1:
        kv_ref = refs[-1]
        at = 0
        for ref in pieces:
            kv_ref[:, :, at : at + ref.shape[2]] = ref[...]
            at += ref.shape[2]
    else:
        kv_ref = pieces[0]
    nt = (((1,), (1,)), ((), ()))
    results = []
    for head in range(kv_ref.shape[1]):
        query = jnp.concatenate([ref[head] for ref in queries], axis=0)
        score = lax.dot_general(query, kv_ref[0, head], nt, preferred_element_type=F32)
        top = jnp.max(score, axis=1, keepdims=True)
        probs = jnp.exp2(score - top).astype(BF16)
        mixed = jnp.dot(probs, kv_ref[1, head], preferred_element_type=F32)
        results.append(mixed[:, :HD] / mixed[:, HD : HD + 1])
    rows = jnp.concatenate(results, axis=1).astype(BF16)
    for chip in range(chips):
        block = rows[chip * capacity : (chip + 1) * capacity]

        def write(first, value):
            out_ref[chip, first : first + value.shape[0]] = value

        pack(block, write)


def attend(queries, pieces, chips, capacity):
    head_count, rows = queries[0].shape[0], chips * capacity
    keys = sum(piece.shape[2] for piece in pieces)
    out_rows = packed_rows(capacity, head_count * HD)[0]
    out_shape = [jax.ShapeDtypeStruct((chips, out_rows, LANE), BF16)]
    if len(pieces) > 1:
        out_shape.append(jax.ShapeDtypeStruct((2, head_count, keys, LANE), BF16))
    made = pl.pallas_call(
        functools.partial(attend_kernel, chips, capacity, len(queries), len(pieces)),
        in_specs=[vmem()] * (len(queries) + len(pieces)),
        out_specs=[vmem()] * len(out_shape),
        out_shape=out_shape,
        cost_estimate=pl.CostEstimate(
            flops=4 * head_count * rows * keys * LANE,
            bytes_accessed=4 * head_count * keys * LANE,
            transcendentals=head_count * rows * keys,
        ),
        compiler_params=limit(24),
        name="attend",
    )(*queries, *pieces)
    return made[0], (made[1] if len(pieces) > 1 else pieces[0])


def finish_kernel(capacity, chips, rounds, index, raw_ref, pick_ref, mod_ref, w_out, w_fc1, w_fc2, *refs):
    parts, earlier, out_ref, whole = refs[:chips], refs[chips:-2], refs[-2], refs[-1]
    members = rounds[index]
    width = raw_ref.shape[1]
    plane, here = coordinates()
    for chip, part in enumerate(parts):
        whole[here ^ chip] = part[...]

    def per_slot(column):
        rows = [mod_ref[column, pl.ds(bag ^ plane, 1)] for bag in members]
        return jnp.concatenate([jnp.broadcast_to(row, (capacity, width)) for row in rows], axis=0)

    attended = jnp.concatenate(
        [
            jnp.concatenate(
                [unpack(whole[chip, at], capacity, width // chips) for chip in range(chips)], axis=1
            )
            for at in range(len(members))
        ],
        axis=0,
    )
    residual = jnp.concatenate(
        [raw_ref[bag * capacity : (bag + 1) * capacity] for bag in members], axis=0
    ).astype(F32)
    branch = jnp.dot(attended, w_out[...], preferred_element_type=F32)
    hidden = (residual + per_slot(2) * branch).astype(BF16)
    normed = (layer_norm(hidden.astype(F32)) * (1.0 + per_slot(4)) + per_slot(3)).astype(BF16)
    active = jax.nn.gelu(jnp.dot(normed, w_fc1[...], preferred_element_type=F32), approximate=True)
    last = jnp.dot(active.astype(BF16), w_fc2[...], preferred_element_type=F32)
    slots = (hidden.astype(F32) + per_slot(5) * last).astype(BF16)
    if index < len(rounds) - 1:
        out_ref[...] = slots
        return
    blocks = {}
    for bags, value in zip(rounds, [ref[...] for ref in earlier] + [slots]):
        for at, bag in enumerate(bags):
            blocks[bag] = value[at * capacity : (at + 1) * capacity]
    slots = jnp.concatenate([blocks[bag] for bag in range(len(blocks))], axis=0)
    tn = (((0,), (0,)), ((), ()))
    out_ref[...] = lax.dot_general(pick_ref[...], slots, tn, preferred_element_type=F32).astype(BF16)


def finish(raw, pick, modulation, parts, earlier, rounds, index, w_out, w_fc1, w_fc2, capacity):
    chips, slot_count = len(parts), capacity * len(rounds[index])
    final = index == len(rounds) - 1
    width, depth, row_count = raw.shape[1], w_fc1.shape[1], pick.shape[1]
    return pl.pallas_call(
        functools.partial(finish_kernel, capacity, chips, rounds, index),
        in_specs=[vmem()] * (6 + chips + len(earlier)),
        out_specs=vmem(),
        out_shape=jax.ShapeDtypeStruct((row_count if final else slot_count, width), BF16),
        scratch_shapes=[pltpu.VMEM((chips,) + parts[0].shape, BF16)],
        cost_estimate=pl.CostEstimate(
            flops=2 * slot_count * width * (width + 2 * depth),
            bytes_accessed=2 * width * (width + 2 * depth),
            transcendentals=slot_count * depth,
        ),
        compiler_params=limit(20),
        name="finish",
    )(raw, pick, modulation, w_out, w_fc1, w_fc2, *parts, *earlier)


def attended_together(bags):
    middle = list(reversed(range(1, bags - 1)))
    return [[bags - 1]] + [middle[at : at + 2] for at in range(0, len(middle), 2)] + [[0]]


def layer(tokens, row_seq, modulation, w_qkv, w_out, w_fc1, w_fc2):
    bags, sp = lax.axis_size("bag"), lax.axis_size("sp")
    along, across, cores = sp // bags, bags // 2, 2
    chips = across * along
    row_count, width = tokens.shape
    capacity = row_count // bags * 5 // 4
    head_count = width // HD // chips

    def swap(value, dx=0, core=0, dz=0, dy=0):
        pairs = []
        for b in range(bags):
            for s in range(sp):
                b2 = ((b // cores) ^ dx) * cores + ((b % cores) ^ core)
                s2 = ((s // along) ^ dz) * along + ((s % along) ^ dy)
                pairs.append((b * sp + s, b2 * sp + s2))
        return lax.ppermute(value, AXES, pairs)

    seq_row = row_seq.reshape(1, row_count)
    modulation = jnp.transpose(modulation, (1, 0, 2))

    def in_place(value):
        return pltpu.with_memory_space_constraint(value, pltpu.HBM)

    inputs = [in_place(value) for value in (tokens, seq_row, modulation)]
    raw, pick, blocks = slot_rows(*inputs, bags, capacity)
    weights = chip_weights(in_place(w_qkv), head_count * HD)
    blocks = [block if k == 0 else swap(block, dz=k) for k, block in enumerate(blocks)]
    halves = round_up(capacity, 32) // 2, capacity - round_up(capacity, 32) // 2
    queries, pieces = [], []
    for k, block in enumerate(blocks):
        if across == 2 and along == 2:
            half = halves[k % 2]
            from_x, from_y = swap(block, dx=1), swap(block, dy=1)
            upper, lower = swap(from_x[:half], dy=1), swap(from_y[half:], dx=1)
            parts = [block, from_y, from_x, upper, lower]
        else:
            parts = [swap(block, dx=j // along, dy=j % along) if j else block for j in range(chips)]
        groups = [parts]
        if k == bags - 1 and len(parts) > chips:
            groups = [parts[: chips - 1], parts[chips - 1 :]]
        queries.append([])
        for group in groups:
            query, kv = project(group, weights, head_count)
            queries[k].append(query)
            pieces += [kv, swap(kv, core=1)]
    mixed = [None] * bags
    rounds = [[bags - 1, 0], list(range(1, bags - 1))] if bags > 2 else [list(range(bags))]

    def exchange(index):
        shares = {}
        for j in reversed(range(chips)):
            share = jnp.stack([mixed[k][j] for k in rounds[index]])
            shares[j] = swap(share, dx=j // along, dy=j % along) if j else share
        return [shares[j] for j in range(chips)]

    for members in attended_together(bags):
        asked = [query for k in members for query in queries[k]]
        part, kv = attend(asked, pieces, chips * len(members), capacity)
        pieces = [kv]
        for at, k in enumerate(members):
            share = part[at * chips : (at + 1) * chips]
            share = swap(share, dz=k) if k else share
            mixed[k] = [share[j] for j in range(chips)]
    shares = [exchange(index) for index in range(len(rounds))]
    done = []
    for index in range(len(rounds)):
        done.append(
            finish(
                raw, pick, modulation, shares[index], done, rounds, index, w_out, w_fc1, w_fc2, capacity
            )
        )
    return done[-1]


def solution(mesh):
    placed = (P(("bag", "sp"), None), P(("bag", "sp")), P(), P(), P(), P(), P())
    return jax.shard_map(layer, mesh=mesh, in_specs=placed, out_specs=P(("bag", "sp"), None), check_vma=False)
```
